512 devices in a mesh: clus: 64 (over x, z, core), samp: 8 (over y).
Axes of the slice: x: 4, y: 8, z: 8, core: 2. Of those that a mesh axis runs over, the one named last changes fastest.
Arguments:
- currents: bfloat16 [2048, 128, 128], P('clus'), may hold values from -6 to 6
- radiate: bfloat16 [2048, 2, 256, 128], P(('clus', 'samp')), may hold values from -0.375 to 0.375
- near_blocks: bfloat16 [2048, 10, 2, 128, 128], P(('clus', 'samp')), may hold values from -0.125 to 0.125
- near_cols: int32 [2048, 10], P(('clus', 'samp')), may hold values from 0 to 2047, as said below
- child_slot: int32 [2048], P('clus'), may hold values from 0 to 31, as said below
- interp: bfloat16 [2048, 256], P('samp'), may hold values from -0.375 to 0.375
- shift_angle: float32 [8, 2048], replicated, may hold values from -3.140625 to 3.140625
- far_dev: int32 [256, 16], P('clus'), may hold values from 0 to 63, all different within a row; in each aligned block of 4 rows (0 to 3, 4 to 7, ...) at most 2 rows name the same one
- far_loc: int32 [256, 16], P('clus'), may hold values from 0 to 3
- far_type: int32 [256, 16], P('clus'), may hold values from 0 to 63
- transl: bfloat16 [64, 2, 2048], P(None, None, 'samp'), may hold values from -0.25 to 0.25
Outputs:
- field: bfloat16 [2048, 128, 128], P(('clus', 'samp'))
The draws below stay inside these ranges and needn't reach their ends.
Inputs may be any that keep to these rules, and one draw needn't show every extreme that they name: `near_cols`: row c holds 10 different clusters, the first being c itself; all lie between g * 32 - 8 and (g + 1) * 32 + 7 for g = c // 32. `child_slot`: each aligned block of 32 entries is a permutation of 0 to 31, so every coarser cluster has eight children, one in each octant. `far_dev`: A row names 16 different values; among the 4 rows of one index of clus no value is named by more than 2 rows, a bound that some block reaches.
All inputs are finite; a program needn't handle non-finite values.
Results may differ from the reference program's by a relative error of at most 0.0071.
Values may be sent and summed in bfloat16 or wider, within the bound.
No kernel may reach another device: no remote copies, remote signals or barrier semaphores. Data moves between devices by JAX's collectives and lax.ppermute only.
A program may use at most 128 MiB of HBM per device.

```python
import math
import jax
import jax.numpy as jnp
import numpy as np
from jax import lax

B = 128
R = 64
K2 = 256
K1 = 2048
NN = 10
NT = 64
PG = 4
GROUP = 32
C2 = 2048
P_SIZE = 256
NF = 16
CAP = 2
HALO = 8


def draw_near_cols(key, part):
    width_all = GROUP + 2 * HALO
    cluster_ids = jnp.arange(C2, dtype=jnp.int32)
    group_ids = cluster_ids // GROUP
    offsets = jnp.arange(width_all, dtype=jnp.int32)
    candidates = group_ids[:, None] * GROUP - HALO + offsets[None, :]
    is_valid = (candidates >= 0) & (candidates < C2) & (candidates != cluster_ids[:, None])
    scores = jax.random.randint(key, (C2, width_all), 0, 4096, dtype=jnp.int32) * width_all + offsets[None, :]
    scores = jnp.where(is_valid, scores, 2 ** 30 + offsets[None, :])
    ranked = jnp.argsort(scores, axis=1)[:, :NN - 1].astype(jnp.int32)
    picked = jnp.take_along_axis(candidates, ranked, axis=1)
    return jnp.concatenate([cluster_ids[:, None], picked], axis=1).astype(jnp.int32)


def draw_child_slot(key, part):
    groups = C2 // GROUP
    scores = jax.random.randint(key, (groups, GROUP), 0, 65536, dtype=jnp.int32) * GROUP + jnp.arange(GROUP, dtype=jnp.int32)[None, :]
    return jnp.argsort(scores, axis=1).astype(jnp.int32).reshape(C2)


def set_ends(entries, own_key, least, largest):
    dims = entries.shape
    place = [jax.random.randint(jax.random.fold_in(own_key, axis), (), 0, dims[axis]) for axis in range(len(dims))]
    entries = entries.at[tuple(place)].set(least)
    longest = dims.index(max(dims))
    place[longest] = (place[longest] + 1) % dims[longest]
    return entries.at[tuple(place)].set(largest)


def level_of(key, shape, cuts, least, largest):
    loudness, own = 1.0, jax.random.fold_in(key, 6)
    for axis_at, shards_of in cuts:
        heights = jnp.exp(jax.random.uniform(jax.random.fold_in(own, axis_at), (shards_of,), jnp.float32, least / len(cuts), largest / len(cuts)))
        loudness = loudness * jnp.repeat(heights, shape[axis_at] // shards_of).reshape([-1 if axis == axis_at else 1 for axis in range(len(shape))])
    return loudness


def shared_out(key, own, number, rows, count, top, bound, skew):
    sequence = jax.random.permutation(key, count)
    crowded, ordinary = load_shares(count, rows * top, bound, skew, True), load_shares(count, rows * top, bound, skew, False)
    places = jnp.arange(count)

    def named(lengths, turn):
        used = int((lengths > 0).sum())
        fixed = max(1, used // 4)
        shifted = fixed + (places - fixed + turn * (used - fixed)) % max(1, count - fixed)
        return jnp.zeros((count,), jnp.int32).at[sequence[jnp.where(places < fixed, places, shifted)]].set(jnp.asarray(lengths, jnp.int32))

    lengths = jnp.where(number % 4 == 0, named(crowded, number // 4), named(ordinary, number - number // 4 - 1))
    mixed = jax.random.permutation(jax.random.fold_in(own, 3), count)
    donor, sink = mixed[0:count // 2 * 2:2], mixed[1:count // 2 * 2:2]
    margin = jnp.minimum(lengths[donor] - 1, bound - lengths[sink]) // 2
    margin = jnp.where((donor == sequence[0]) | (sink == sequence[0]) | (lengths[sink] == 0), 0, jnp.maximum(margin, 0))
    shifted = jax.random.randint(jax.random.fold_in(own, 4), (count // 2,), 0, 1 << 20) % (margin + 1)
    lengths = lengths.at[donor].add(-shifted).at[sink].add(shifted)
    labels = jnp.searchsorted(jnp.cumsum(lengths), jnp.arange(rows * top), side="right").astype(jnp.int32)
    listing = labels.reshape(top, rows).T
    listing = listing[jax.random.permutation(jax.random.fold_in(own, 1), rows)]
    turn = jax.random.randint(jax.random.fold_in(own, 2), (rows, 1), 0, top)
    return jnp.take_along_axis(listing, (jnp.arange(top)[None, :] + turn) % top, axis=1)


def load_shares(amount, total, reach, slope, full):
    portions = [(1 << 20) // math.isqrt(standing ** slope) + 1 for standing in range(1, amount + 1)]
    largest = reach if full else min(reach, max(-(-total // amount), total * portions[0] // sum(portions)))
    least = 1 if total - largest >= amount - 1 else 0
    holding, surplus = [largest] + [least] * (amount - 1), total - largest - least * (amount - 1)
    while surplus > 0:
        free = [i for i in range(1, amount) if holding[i] < largest] or [i for i in range(1, amount) if holding[i] < reach]
        whole, left = sum([portions[i] for i in free]), surplus
        for i in free:
            extra = min(reach - holding[i], max(1, left * portions[i] // whole), surplus)
            holding[i] = holding[i] + extra
            surplus = surplus - extra
    return np.array(holding)


def gaussian(stream_key, dims, width, limit, shards=(), kind=jnp.bfloat16):
    array = width * jax.random.normal(stream_key, dims, jnp.float32)
    if shards:
        array = array * level_of(stream_key, dims, shards, -0.22, 0.18)
    return jnp.clip(array, -limit, limit).astype(kind)


def setup_inputs(seed: int = 0) -> dict:
    key_list = jax.random.split(jax.random.key(seed), 12)
    currents = gaussian(key_list[0], (C2, B, 2 * R), 1.0, 6.0, ((0, 64),))
    radiate = gaussian(key_list[1], (C2, 2, K2, B), (2 * B) ** -0.5, 0.375, ((0, 512),))
    near_blocks = gaussian(key_list[2], (C2, NN, 2, B, B), (2 * B * NN) ** -0.5, 0.125, ((0, 512),))
    near_cols = draw_near_cols(jax.random.fold_in(key_list[11], 71), 0)
    child_slot = draw_child_slot(jax.random.fold_in(key_list[11], 71), 0)
    interp = gaussian(key_list[5], (K1, K2), K2 ** -0.5, 0.375, ((0, 8),))
    shift_angle = jnp.clip(jax.random.uniform(key_list[6], (8, K1), jnp.float32, -3.140625, 3.140625), -3.140625, 3.140625)
    far_dev_keys = jax.random.split(jax.random.fold_in(key_list[7], 1), P_SIZE // PG)
    far_dev_turns = jax.random.permutation(jax.random.fold_in(key_list[7], 3), P_SIZE // PG)
    far_dev = jax.vmap(lambda own, number: shared_out(jax.random.fold_in(key_list[7], 2), own, number, PG, P_SIZE // PG, NF, CAP, 2))(far_dev_keys, far_dev_turns).reshape((P_SIZE, NF))
    far_loc = set_ends(jax.random.randint(key_list[8], (P_SIZE, NF), 0, PG), jax.random.fold_in(key_list[8], 1), 0, PG - 1).astype(jnp.int32)
    far_type = set_ends(jax.random.randint(key_list[9], (P_SIZE, NF), 0, NT), jax.random.fold_in(key_list[9], 1), 0, NT - 1).astype(jnp.int32)
    transl = gaussian(key_list[10], (NT, 2, K1), (0.07 / NF ** 0.5), 0.25, ((2, 8),))
    return dict(currents=currents, radiate=radiate, near_blocks=near_blocks, near_cols=near_cols, child_slot=child_slot, interp=interp, shift_angle=shift_angle, far_dev=far_dev, far_loc=far_loc, far_type=far_type, transl=transl)


def rounded(values):
    return lax.optimization_barrier(values.astype(jnp.bfloat16))


def combine_parts(with_real, with_imag, sign):
    half_width = with_real.shape[-1] // 2
    real_part = with_real[..., :half_width] - sign * with_imag[..., half_width:]
    imag_part = with_real[..., half_width:] + sign * with_imag[..., :half_width]
    return jnp.concatenate([real_part, imag_part], axis=-1)


def rotate_parts(values, cosine, sine_part):
    half_width = values.shape[-1] // 2
    real_in = values[..., :half_width]
    imag_in = values[..., half_width:]
    cosine = cosine[..., None]
    sine_part = sine_part[..., None]
    return jnp.concatenate([real_in * cosine - imag_in * sine_part, real_in * sine_part + imag_in * cosine], axis=-1)


def reference(currents, radiate, near_blocks, near_cols, child_slot, interp, shift_angle, far_dev, far_loc, far_type, transl):
    cosine_tab = jnp.cos(shift_angle)
    sine_tab = jnp.sin(shift_angle)
    interp_wide = interp.astype(jnp.float32)
    transl_wide = transl.astype(jnp.float32)
    group_count = C2 // GROUP

    def aggregate(operands):
        matrix, values = operands
        with_real = jnp.dot(matrix[0], values, preferred_element_type=jnp.float32)
        with_imag = jnp.dot(matrix[1], values, preferred_element_type=jnp.float32)
        return combine_parts(with_real, with_imag, 1.0)

    rad_child = rounded(lax.map(aggregate, (radiate, currents)))

    def lift(group_index):
        row_start = group_index * GROUP
        rad_group = lax.dynamic_slice_in_dim(rad_child, row_start, GROUP, 0).astype(jnp.float32)
        slot_ids = lax.dynamic_slice_in_dim(child_slot, row_start, GROUP, 0)
        lifted = jnp.einsum('kj,cjr->ckr', interp_wide, rad_group)
        octants = slot_ids % 8
        rotated = rotate_parts(lifted, cosine_tab[octants], sine_tab[octants])
        owners = (slot_ids[:, None] // 8 == jnp.arange(PG, dtype=jnp.int32)[None, :]).astype(jnp.float32)
        return jnp.einsum('cp,ckr->pkr', owners, rotated, precision=lax.Precision.HIGHEST)

    groups = jnp.arange(group_count, dtype=jnp.int32)
    rad_parent = rounded(lax.map(lift, groups).reshape(P_SIZE, K1, 2 * R))

    partners = (far_dev * PG + far_loc).astype(jnp.int32)

    def translate(list_row):
        part_ids, type_ids = list_row
        blocks = rad_parent[part_ids].astype(jnp.float32)
        operators = transl_wide[type_ids]
        real_in = blocks[..., :R]
        imag_in = blocks[..., R:]
        cosine = operators[:, 0][..., None]
        sine_part = operators[:, 1][..., None]
        real_sum = jnp.sum(real_in * cosine - imag_in * sine_part, axis=0)
        imag_sum = jnp.sum(real_in * sine_part + imag_in * cosine, axis=0)
        return jnp.concatenate([real_sum, imag_sum], axis=-1)

    incoming = rounded(lax.map(translate, (partners, far_type)))

    def descend(group_index):
        slot_ids = lax.dynamic_slice_in_dim(child_slot, group_index * GROUP, GROUP, 0)
        rec_group = lax.dynamic_slice_in_dim(incoming, group_index * PG, PG, 0).astype(jnp.float32)
        chosen = rec_group[slot_ids // 8]
        octants = slot_ids % 8
        phased = rounded(rotate_parts(chosen, cosine_tab[octants], -sine_tab[octants])).astype(jnp.float32)
        return jnp.einsum('kj,ckr->cjr', interp_wide, phased)

    child_in = rounded(lax.map(descend, groups).reshape(C2, K2, 2 * R))

    def finish(cluster_data):
        matrix, blocks, col_ids, received = cluster_data
        with_real = jnp.dot(matrix[0].T, received, preferred_element_type=jnp.float32)
        with_imag = jnp.dot(matrix[1].T, received, preferred_element_type=jnp.float32)
        far_part = combine_parts(with_real, with_imag, -1.0)
        neighbours = currents[col_ids].astype(jnp.float32)
        blocks_wide = blocks.astype(jnp.float32)
        near_real = jnp.einsum('jab,jbr->ar', blocks_wide[:, 0], neighbours)
        near_imag = jnp.einsum('jab,jbr->ar', blocks_wide[:, 1], neighbours)
        near_part = combine_parts(near_real, near_imag, 1.0)
        return (near_part + far_part).astype(jnp.bfloat16)

    return lax.map(finish, (radiate, near_blocks, near_cols, child_in))
```

```python
import jax
import jax.numpy as jnp
from jax import lax
from jax.experimental import pallas as pl
from jax.experimental.pallas import tpu as pltpu
from jax.sharding import PartitionSpec as P

BF = jnp.bfloat16
F32 = jnp.float32
VMEM_LIMIT = 60 * 1024 * 1024
VM = pl.BlockSpec(memory_space=pltpu.VMEM)
SM = pl.BlockSpec(memory_space=pltpu.SMEM)


def nt_dot(a, b):
    return lax.dot_general(a, b, (((1,), (1,)), ((), ())), preferred_element_type=F32)


def nn_dot(a, b):
    return lax.dot_general(a, b, (((1,), (0,)), ((), ())), preferred_element_type=F32)


def tn_dot(a, b):
    return lax.dot_general(a, b, (((0,), (0,)), ((), ())), preferred_element_type=F32)


def rows_of(shape, dim):
    return lax.broadcasted_iota(jnp.int32, shape, dim)


def radiate_kernel(ids, cur, rad, itp, tra, lists, out):
    trow = tra[0].astype(F32)
    row = rows_of((8, 256), 0)
    extra = jnp.where(row == 0, trow[0:1], jnp.where(row == 1, trow[1:2], lists[...]))
    extra = extra.astype(BF)
    for s in range(8):
        out[s, 64:192, :] = itp[...]
        out[s, 192:200, :] = extra
    for c in range(4):
        values = cur[c].astype(F32).T.astype(BF)
        with_real = nt_dot(values, rad[c, 0])
        with_imag = nt_dot(values, rad[c, 1])
        real = with_real[:64] - with_imag[64:]
        imag = with_real[64:] + with_imag[:64]
        for s in range(8):
            both = jnp.concatenate([real[8 * s : 8 * s + 8], imag[8 * s : 8 * s + 8]], axis=0)
            out[s, 16 * c : 16 * c + 16, :] = both.astype(BF)


def lift_kernel(slots, ids, got, other, cosine, sine, out, whole, lhs, inverse):
    core = ids[0]

    def note(c, carry):
        inverse[slots[c]] = c
        return carry

    lax.fori_loop(0, 32, note, 0)

    def collect(n, carry):
        c = inverse[n]
        src = pl.multiple_of(lax.rem(c, 4) * 16, 16)
        dst = pl.multiple_of(n * 16, 16)
        lhs[pl.ds(dst, 16), :] = got[lax.div(c, 4), pl.ds(src, 16), :]
        return carry

    lax.fori_loop(0, 32, collect, 0)
    mine = pl.multiple_of(core * 128, 128)
    theirs = pl.multiple_of((1 - core) * 128, 128)
    for s in range(8):
        whole[s, pl.ds(mine, 128), :] = got[s, 64:192, :]
        whole[s, pl.ds(theirs, 128), :] = other[s]

    def step(k, carry):
        lanes = pl.ds(pl.multiple_of(k * 256, 256), 256)
        cos = cosine[:, lanes]
        sin = sine[:, lanes]
        for p in range(4):
            lifted = nt_dot(lhs[128 * p : 128 * p + 128, :], whole[k])
            real_sum = imag_sum = None
            for o in range(8):
                re = lifted[16 * o : 16 * o + 8]
                im = lifted[16 * o + 8 : 16 * o + 16]
                co, si = cos[o : o + 1], sin[o : o + 1]
                real = re * co - im * si
                imag = re * si + im * co
                real_sum = real if real_sum is None else real_sum + real
                imag_sum = imag if imag_sum is None else imag_sum + imag
            parts = (real_sum, imag_sum)
            if p == 0:
                reals, imags = [], []
            reals.append(parts[0])
            imags.append(parts[1])
        block = jnp.stack(reals + imags, axis=0)
        block = jnp.swapaxes(block, 0, 1)
        extra = got[k, 192:208, :].astype(F32)[0:8]
        extra = jnp.broadcast_to(extra[None], (8, 8, 256))
        both = jnp.concatenate([block, extra], axis=1).astype(BF)
        for r in range(8):
            out[r // 2, k, r % 2] = both[r]
        return carry

    lax.fori_loop(0, 8, step, 0)


def translate_kernel(got, out, table, tran, codes, real_acc, imag_acc):
    table[...] = got[:, 0:8, :].reshape(512, 256)
    tran[...] = got[:, 8:16, :].reshape(512, 256)
    row = rows_of((256, 512), 0)
    col = rows_of((256, 512), 1)
    pick = (col == (lax.shift_right_logical(row, 2) * 8 + 2 + (row & 3))).astype(F32).astype(BF)
    listed = nn_dot(pick, tran[:, 0:128])
    codes[...] = listed.astype(jnp.int32)
    real_acc[...] = jnp.zeros_like(real_acc)
    imag_acc[...] = jnp.zeros_like(imag_acc)
    for f in range(16):
        code = codes[:, f : f + 1]
        src = code + lax.shift_right_logical(code, 2) * 4
        kind = codes[:, 16 + f : 17 + f] * 8
        one = lambda target: (col == target).astype(F32).astype(BF)
        re = nn_dot(one(src), table[...])
        im = nn_dot(one(src + 4), table[...])
        tre = nn_dot(one(kind), tran[...])
        tim = nn_dot(one(kind + 1), tran[...])
        real_acc[...] += re * tre - im * tim
        imag_acc[...] += re * tim + im * tre
    re = real_acc[...].reshape(32, 8, 256)
    im = imag_acc[...].reshape(32, 8, 256)
    low = rows_of((32, 8, 256), 1) < 4
    out[:, 0] = jnp.where(low, re, pltpu.roll(im, 4, 1)).astype(BF)
    out[:, 1] = jnp.where(low, pltpu.roll(re, 4, 1), im).astype(BF)


def descend_kernel(slots, got, cosine, sine, whole, out, lhs, acc):
    acc[...] = jnp.zeros_like(acc)

    def step(k, carry):
        lanes = pl.ds(pl.multiple_of(k * 256, 256), 256)
        cos = cosine[:, lanes]
        sin = sine[:, lanes]
        block = jnp.stack([got[r // 2, k, r % 2].astype(F32) for r in range(8)], axis=0)
        block = jnp.swapaxes(block, 0, 1)
        for p in range(4):
            re, im = block[p], block[4 + p]
            for o in range(8):
                co, si = cos[o : o + 1], sin[o : o + 1]
                both = jnp.concatenate([re * co + im * si, im * co - re * si], axis=0)
                n = 8 * p + o
                lhs[16 * n : 16 * n + 16, :] = both.astype(BF)
        acc[...] += nn_dot(lhs[...], whole[k])
        return carry

    lax.fori_loop(0, 8, step, 0)

    def place(c, carry):
        src = pl.multiple_of(slots[c] * 16, 16)
        dst = pl.multiple_of(lax.rem(c, 4) * 16, 16)
        out[lax.div(c, 4), pl.ds(dst, 16), :] = acc[pl.ds(src, 16), :].astype(BF)
        return carry

    lax.fori_loop(0, 32, place, 0)


def finish_kernel(got, rad, near, out):
    for c in range(4):
        pieces = [got[s, 16 * c : 16 * c + 16, :].astype(F32) for s in range(8)]
        rows = jnp.concatenate([q[:8] for q in pieces] + [q[8:] for q in pieces], axis=0)
        received = rows.T.astype(BF)
        with_real = tn_dot(rad[c, 0], received)
        with_imag = tn_dot(rad[c, 1], received)
        turned = pltpu.roll(with_imag, 64, 1)
        lane = rows_of((128, 128), 1)
        far = with_real + jnp.where(lane < 64, turned, -turned)
        out[c] = (near[c] + far).astype(BF)


def params():
    return pltpu.CompilerParams(vmem_limit_bytes=VMEM_LIMIT)


def combine_parts(with_real, with_imag, sign):
    half_width = with_real.shape[-1] // 2
    real_part = with_real[..., :half_width] - sign * with_imag[..., half_width:]
    imag_part = with_real[..., half_width:] + sign * with_imag[..., :half_width]
    return jnp.concatenate([real_part, imag_part], axis=-1)


def near_field(currents, near_blocks, near_cols):
    group = currents.shape[0]
    margin = group // 4
    count = lax.axis_size("clus")
    up = [(i, i + 1) for i in range(count - 1)]
    down = [(b, a) for a, b in up]
    low = lax.ppermute(currents[group - margin :], "clus", up)
    high = lax.ppermute(currents[:margin], "clus", down)
    window = jnp.concatenate([low, currents, high], axis=0)
    local = near_cols - (lax.axis_index("clus") * group - margin)
    neighbours = window[local]
    near_real = jnp.einsum(
        "cjab,cjbr->car", near_blocks[:, :, 0], neighbours, preferred_element_type=F32
    )
    near_imag = jnp.einsum(
        "cjab,cjbr->car", near_blocks[:, :, 1], neighbours, preferred_element_type=F32
    )
    return combine_parts(near_real, near_imag, 1.0)


def body(
    currents,
    radiate,
    near_blocks,
    near_cols,
    child_slot,
    interp,
    shift_angle,
    far_dev,
    far_loc,
    far_type,
    transl,
):
    samp = lax.axis_index("samp")
    clus = lax.axis_index("clus")
    core = lax.rem(clus, 2)
    ids = jnp.stack([core, samp, clus]).astype(jnp.int32)
    partner = [(i, i ^ 1) for i in range(lax.axis_size("clus"))]
    codes = (far_dev * 4 + far_loc).astype(F32)
    kinds = far_type.astype(F32)
    lists = jnp.pad(codes, ((2, 2), (0, 240))) + jnp.pad(kinds, ((2, 2), (16, 224)))
    cosine = jnp.cos(shift_angle)
    sine = jnp.sin(shift_angle)

    sent = pl.pallas_call(
        radiate_kernel,
        name="radiate",
        out_shape=jax.ShapeDtypeStruct((8, 208, 256), BF),
        grid_spec=pltpu.PrefetchScalarGridSpec(
            num_scalar_prefetch=1,
            grid=(1,),
            in_specs=[
                pl.BlockSpec((4, 128, 128), lambda i, ids: (ids[1], 0, 0)),
                pl.BlockSpec((4, 2, 256, 128), lambda i, ids: (0, 0, 0, 0)),
                pl.BlockSpec((128, 256), lambda i, ids: (ids[0], 0)),
                pl.BlockSpec((1, 2, 256), lambda i, ids: (ids[2], 0, 0)),
                pl.BlockSpec((8, 256), lambda i, ids: (0, 0)),
            ],
            out_specs=pl.BlockSpec((8, 208, 256), lambda i, ids: (0, 0, 0)),
        ),
        compiler_params=params(),
    )(ids, currents, radiate, interp, transl, lists)
    got = lax.all_to_all(sent, "samp", split_axis=0, concat_axis=0, tiled=True)
    other = lax.ppermute(got[:, 64:192], "clus", partner)

    sent, whole = pl.pallas_call(
        lift_kernel,
        name="lift",
        out_shape=(
            jax.ShapeDtypeStruct((4, 8, 2, 16, 256), BF),
            jax.ShapeDtypeStruct((8, 256, 256), BF),
        ),
        in_specs=[SM, SM, VM, VM, VM, VM],
        out_specs=(VM, VM),
        scratch_shapes=[pltpu.VMEM((512, 256), BF), pltpu.SMEM((32,), jnp.int32)],
        compiler_params=params(),
    )(child_slot, ids, got, other, cosine, sine)
    got = lax.all_to_all(
        sent.reshape(64, 16, 256), "clus", split_axis=0, concat_axis=0, tiled=True
    )

    sent = pl.pallas_call(
        translate_kernel,
        name="translate",
        out_shape=jax.ShapeDtypeStruct((32, 2, 8, 256), BF),
        in_specs=[VM],
        out_specs=VM,
        scratch_shapes=[
            pltpu.VMEM((512, 256), BF),
            pltpu.VMEM((512, 256), BF),
            pltpu.VMEM((256, 128), jnp.int32),
            pltpu.VMEM((256, 256), F32),
            pltpu.VMEM((256, 256), F32),
        ],
        compiler_params=params(),
    )(got)
    got = lax.all_to_all(
        sent.reshape(64, 8, 256), "clus", split_axis=0, concat_axis=0, tiled=True
    )

    sent = pl.pallas_call(
        descend_kernel,
        name="descend",
        out_shape=jax.ShapeDtypeStruct((8, 64, 256), BF),
        in_specs=[SM, VM, VM, VM, VM],
        out_specs=VM,
        scratch_shapes=[pltpu.VMEM((512, 256), BF), pltpu.VMEM((512, 256), F32)],
        compiler_params=params(),
    )(child_slot, got.reshape(4, 8, 2, 8, 256), cosine, sine, whole)
    got = lax.all_to_all(sent, "samp", split_axis=0, concat_axis=0, tiled=True)

    near = near_field(currents, near_blocks, near_cols)
    return pl.pallas_call(
        finish_kernel,
        name="finish",
        out_shape=jax.ShapeDtypeStruct((4, 128, 128), BF),
        in_specs=[VM, VM, VM],
        out_specs=VM,
        compiler_params=params(),
    )(got, radiate, near)


def solution(mesh):
    in_specs = (
        P("clus", None, None),
        P(("clus", "samp"), None, None, None),
        P(("clus", "samp"), None, None, None, None),
        P(("clus", "samp"), None),
        P("clus"),
        P("samp", None),
        P(),
        P("clus", None),
        P("clus", None),
        P("clus", None),
        P(None, None, "samp"),
    )
    out_specs = P(("clus", "samp"), None, None)
    return jax.shard_map(body, mesh=mesh, in_specs=in_specs, out_specs=out_specs, check_vma=False)
```

```python
import jax
import jax.numpy as jnp
from jax import lax
from jax.experimental import pallas as pl
from jax.experimental.pallas import tpu as pltpu
from jax.sharding import PartitionSpec as P

BF = jnp.bfloat16
F32 = jnp.float32
VMEM_LIMIT = 16 * 1024 * 1024
VM = pl.BlockSpec(memory_space=pltpu.VMEM)
SM = pl.BlockSpec(memory_space=pltpu.SMEM)


def nt_dot(a, b):
    return lax.dot_general(a, b, (((1,), (1,)), ((), ())), preferred_element_type=F32)


def nn_dot(a, b):
    return lax.dot_general(a, b, (((1,), (0,)), ((), ())), preferred_element_type=F32)


def tn_dot(a, b):
    return lax.dot_general(a, b, (((0,), (0,)), ((), ())), preferred_element_type=F32)


def rows_of(shape, dim):
    return lax.broadcasted_iota(jnp.int32, shape, dim)


def radiate_kernel(cur, rad_all, itp, tra, out, own, rad, half_ref, tran, sems):
    clus = lax.axis_index("clus")
    mine = pl.ds(pl.multiple_of(lax.rem(clus, 2) * 128, 128), 128)
    pairs = [
        (itp.at[mine], half_ref),
        (tra.at[clus], tran),
        (cur.at[pl.ds(lax.axis_index("samp") * 4, 4)], own),
    ] + [(rad_all.at[c], rad.at[c]) for c in range(4)]
    copies = [pltpu.make_async_copy(a, b, sems.at[i]) for i, (a, b) in enumerate(pairs)]
    for copy in copies:
        copy.start()
    copies[0].wait()
    copies[1].wait()
    half = half_ref[...]
    trow = tran[...].astype(F32)
    row = rows_of((8, 256), 0)
    extra = jnp.where(row == 0, trow[0:1], jnp.where(row == 1, trow[1:2], 0.0)).astype(BF)
    for s in range(8):
        out[s, 64:192, :] = half
        out[s, 192:200, :] = extra
    copies[2].wait()
    for c in range(4):
        copies[3 + c].wait()
        values = own[c].astype(F32).T.astype(BF)
        with_real = nt_dot(values, rad[c, 0])
        with_imag = nt_dot(values, rad[c, 1])
        real = with_real[:64] - with_imag[64:]
        imag = with_real[64:] + with_imag[:64]
        for s in range(8):
            both = jnp.concatenate([real[8 * s : 8 * s + 8], imag[8 * s : 8 * s + 8]], axis=0)
            out[s, 16 * c : 16 * c + 16, :] = both.astype(BF)


def own_lanes(k):
    core = lax.rem(lax.axis_index("clus"), 2)
    return pl.ds(pl.multiple_of(k * 256 + core * 128, 128), 128)


def other_lanes(k):
    core = lax.rem(lax.axis_index("clus"), 2)
    return pl.ds(pl.multiple_of(k * 256 + (1 - core) * 128, 128), 128)


def lift_half(rows, matrix, cos, sin):
    reals, imags = [], []
    for p in range(4):
        lifted = nt_dot(rows[128 * p : 128 * p + 128, :], matrix)
        real_sum = imag_sum = None
        for o in range(8):
            re = lifted[16 * o : 16 * o + 8]
            im = lifted[16 * o + 8 : 16 * o + 16]
            co, si = cos[o : o + 1], sin[o : o + 1]
            real = re * co - im * si
            imag = re * si + im * co
            real_sum = real if real_sum is None else real_sum + real
            imag_sum = imag if imag_sum is None else imag_sum + imag
        reals.append(real_sum)
        imags.append(imag_sum)
    return jnp.swapaxes(jnp.stack(reals + imags, axis=0), 0, 1).astype(BF)


def lift_own_kernel(slots, got, cosine, sine, out, rows, inverse):
    def note(c, carry):
        inverse[slots[c]] = c
        return carry

    lax.fori_loop(0, 32, note, 0)

    def collect(n, carry):
        c = inverse[n]
        src = pl.multiple_of(lax.rem(c, 4) * 16, 16)
        dst = pl.multiple_of(n * 16, 16)
        rows[pl.ds(dst, 16), :] = got[lax.div(c, 4), pl.ds(src, 16), :]
        return carry

    lax.fori_loop(0, 32, collect, 0)

    def step(k, carry):
        lanes = own_lanes(k)
        block = lift_half(rows, got[k, 64:192, :], cosine[:, lanes], sine[:, lanes])
        for r in range(8):
            out[r // 2, k, r % 2] = block[r]
        return carry

    lax.fori_loop(0, 8, step, 0)


def lift_other_kernel(first, rows, got, other, lists, cosine, sine, out):
    row = rows_of((8, 128), 0)

    def step(k, carry):
        lanes = other_lanes(k)
        block = lift_half(rows, other[k], cosine[:, lanes], sine[:, lanes])
        tran = got[k, 192:200, :].astype(F32)
        tile = lists[...]
        for j in range(4):
            piece = tran[j // 2 : j // 2 + 1, 128 * (j % 2) : 128 * (j % 2) + 128]
            tile = jnp.where(row == 4 + j, piece, tile)
        tile = tile.astype(BF)
        for r in range(8):
            out[r // 2, k, r % 2, :, 0:128] = first[r // 2, k, r % 2]
            out[r // 2, k, r % 2, :, 128:256] = block[r]
            out[r // 2, k, r % 2, :, 256:384] = tile
        return carry

    lax.fori_loop(0, 8, step, 0)


def translate_kernel(got, out, table, codes, tran, real_acc, imag_acc):
    def uppers(even, odd):
        low = rows_of(even.shape, 1) < 4
        return jnp.where(low, even, pltpu.roll(odd, 4, 1)).reshape(256, even.shape[2])

    def lowers(even, odd):
        low = rows_of(even.shape, 1) < 4
        return jnp.where(low, pltpu.roll(even, 4, 1), odd).reshape(256, even.shape[2])

    for h in range(2):
        even = got[:, 0, :, 128 * h : 128 * h + 128].astype(F32)
        odd = got[:, 1, :, 128 - 128 * h : 256 - 128 * h].astype(F32)
        table[:, 128 * h : 128 * h + 128] = uppers(even, odd).astype(BF)
        table[:, 256 + 128 * h : 384 + 128 * h] = lowers(even, odd).astype(BF)
    even = got[:, 0, :, 256:384].astype(F32)
    odd = got[:, 1, :, 256:384].astype(F32)
    codes[...] = uppers(even, odd).astype(jnp.int32)
    pieces = lowers(even, odd).astype(BF)
    for j in range(4):
        pick = rows_of((64, 256), 1) == rows_of((64, 256), 0) * 4 + j
        part = nn_dot(pick.astype(F32).astype(BF), pieces)
        tran[:, 128 * j : 128 * j + 128] = part.astype(BF)
    col = rows_of((256, 256), 1)
    kinds = rows_of((256, 64), 1)
    for f in range(16):
        pick = (col == codes[:, f : f + 1]).astype(F32).astype(BF)
        kind = (kinds == codes[:, 16 + f : 17 + f]).astype(F32).astype(BF)
        both = nn_dot(pick, table[...])
        factor = nn_dot(kind, tran[...])
        re, im = both[:, :256], both[:, 256:]
        tre, tim = factor[:, :256], factor[:, 256:]
        real = re * tre - im * tim
        imag = re * tim + im * tre
        if f == 0:
            real_acc[...] = real
            imag_acc[...] = imag
        else:
            real_acc[...] += real
            imag_acc[...] += imag
    low = rows_of((32, 8, 256), 1) < 4
    re = real_acc[...].reshape(32, 8, 256)
    im = imag_acc[...].reshape(32, 8, 256)
    out[:, 0] = jnp.where(low, re, pltpu.roll(im, 4, 1)).astype(BF)
    last = jnp.where(low, pltpu.roll(re, 4, 1), im).astype(BF)
    out[:, 1, :, 0:128] = last[:, :, 128:256]
    out[:, 1, :, 128:256] = last[:, :, 0:128]


def descend_kernel(slots, got, half, other, cosine, sine, out, lhs, acc):
    acc[...] = jnp.zeros_like(acc)

    def step(k, carry):
        mine, theirs = own_lanes(k), other_lanes(k)
        cos = jnp.concatenate([cosine[:, mine], cosine[:, theirs]], axis=1)
        sin = jnp.concatenate([sine[:, mine], sine[:, theirs]], axis=1)
        block = jnp.stack([got[r // 2, k, r % 2].astype(F32) for r in range(8)], axis=0)
        block = jnp.swapaxes(block, 0, 1)
        for p in range(4):
            re, im = block[p], block[4 + p]
            for o in range(8):
                co, si = cos[o : o + 1], sin[o : o + 1]
                both = jnp.concatenate([re * co + im * si, im * co - re * si], axis=0)
                n = 8 * p + o
                lhs[16 * n : 16 * n + 16, :] = both.astype(BF)
        whole = jnp.concatenate([half[k], other[k]], axis=0)
        acc[...] += nn_dot(lhs[...], whole)
        return carry

    lax.fori_loop(0, 8, step, 0)

    def place(c, carry):
        src = pl.multiple_of(slots[c] * 16, 16)
        dst = pl.multiple_of(lax.rem(c, 4) * 16, 16)
        out[lax.div(c, 4), pl.ds(dst, 16), :] = acc[pl.ds(src, 16), :].astype(BF)
        return carry

    lax.fori_loop(0, 32, place, 0)


def finish_kernel(got, rad, near, out):
    for c in range(4):
        pieces = [got[s, 16 * c : 16 * c + 16, :].astype(F32) for s in range(8)]
        rows = jnp.concatenate([q[:8] for q in pieces] + [q[8:] for q in pieces], axis=0)
        received = rows.T.astype(BF)
        with_real = tn_dot(rad[c, 0], received)
        with_imag = tn_dot(rad[c, 1], received)
        turned = pltpu.roll(with_imag, 64, 1)
        lane = rows_of((128, 128), 1)
        far = with_real + jnp.where(lane < 64, turned, -turned)
        out[c] = (near[c] + far).astype(BF)


def params(limit=VMEM_LIMIT):
    return pltpu.CompilerParams(vmem_limit_bytes=limit)


def combine_parts(with_real, with_imag, sign):
    half_width = with_real.shape[-1] // 2
    real_part = with_real[..., :half_width] - sign * with_imag[..., half_width:]
    imag_part = with_real[..., half_width:] + sign * with_imag[..., :half_width]
    return jnp.concatenate([real_part, imag_part], axis=-1)


def near_field(currents, near_blocks, near_cols):
    group = currents.shape[0]
    margin = group // 4
    count = lax.axis_size("clus")
    up = [(i, i + 1) for i in range(count - 1)]
    down = [(b, a) for a, b in up]
    low = lax.ppermute(currents[group - margin :], "clus", up)
    high = lax.ppermute(currents[:margin], "clus", down)
    window = jnp.concatenate([low, currents, high], axis=0)
    local = near_cols - (lax.axis_index("clus") * group - margin)
    neighbours = window[local]
    near_real = jnp.einsum(
        "cjab,cjbr->car", near_blocks[:, :, 0], neighbours, preferred_element_type=F32
    )
    near_imag = jnp.einsum(
        "cjab,cjbr->car", near_blocks[:, :, 1], neighbours, preferred_element_type=F32
    )
    return combine_parts(near_real, near_imag, 1.0)


def body(
    currents,
    radiate,
    near_blocks,
    near_cols,
    child_slot,
    interp,
    shift_angle,
    far_dev,
    far_loc,
    far_type,
    transl,
):
    partner = [(i, i ^ 1) for i in range(lax.axis_size("clus"))]
    exchange = lambda x, axis: lax.all_to_all(x, axis, split_axis=0, concat_axis=0, tiled=True)
    lists = jnp.pad((far_dev * 4 + far_loc).astype(F32), ((0, 4), (0, 112)))
    lists = lists + jnp.pad(far_type.astype(F32), ((0, 4), (16, 96)))
    cosine = jnp.cos(shift_angle)
    sine = jnp.sin(shift_angle)

    sent = pl.pallas_call(
        radiate_kernel,
        name="radiate",
        out_shape=jax.ShapeDtypeStruct((8, 200, 256), BF),
        in_specs=[pl.BlockSpec(memory_space=pltpu.HBM)] * 4,
        out_specs=VM,
        scratch_shapes=[
            pltpu.VMEM((4, 128, 128), BF),
            pltpu.VMEM((4, 2, 256, 128), BF),
            pltpu.VMEM((128, 256), BF),
            pltpu.VMEM((2, 256), BF),
            pltpu.SemaphoreType.DMA((7,)),
        ],
        compiler_params=params(60 * 1024 * 1024),
    )(currents, radiate, interp, transl)
    got = exchange(sent, "samp")
    half = got[:, 64:192]
    other = lax.ppermute(half, "clus", partner)

    first, rows = pl.pallas_call(
        lift_own_kernel,
        name="lift_own",
        out_shape=(
            jax.ShapeDtypeStruct((4, 8, 2, 8, 128), BF),
            jax.ShapeDtypeStruct((512, 256), BF),
        ),
        in_specs=[SM, VM, VM, VM],
        out_specs=(VM, VM),
        scratch_shapes=[pltpu.SMEM((32,), jnp.int32)],
        compiler_params=params(),
    )(child_slot, got, cosine, sine)
    sent = pl.pallas_call(
        lift_other_kernel,
        name="lift_other",
        out_shape=jax.ShapeDtypeStruct((4, 8, 2, 8, 384), BF),
        in_specs=[VM] * 7,
        out_specs=VM,
        compiler_params=params(),
    )(first, rows, got, other, lists, cosine, sine)
    moved = exchange(sent.reshape(64, 8, 384), "clus")

    sent = pl.pallas_call(
        translate_kernel,
        name="translate",
        out_shape=jax.ShapeDtypeStruct((32, 2, 8, 256), BF),
        in_specs=[VM],
        out_specs=VM,
        scratch_shapes=[
            pltpu.VMEM((256, 512), BF),
            pltpu.VMEM((256, 128), jnp.int32),
            pltpu.VMEM((64, 512), BF),
            pltpu.VMEM((256, 256), F32),
            pltpu.VMEM((256, 256), F32),
        ],
        compiler_params=params(),
    )(moved.reshape(32, 2, 8, 384))
    moved = exchange(sent.reshape(64, 8, 256), "clus")

    sent = pl.pallas_call(
        descend_kernel,
        name="descend",
        out_shape=jax.ShapeDtypeStruct((8, 64, 256), BF),
        in_specs=[SM, VM, VM, VM, VM, VM],
        out_specs=VM,
        scratch_shapes=[
            pltpu.VMEM((512, 256), BF),
            pltpu.VMEM((512, 256), F32),
        ],
        compiler_params=params(),
    )(child_slot, moved.reshape(4, 8, 2, 8, 256), half, other, cosine, sine)
    got = exchange(sent, "samp")

    near = near_field(currents, near_blocks, near_cols)
    return pl.pallas_call(
        finish_kernel,
        name="finish",
        out_shape=jax.ShapeDtypeStruct((4, 128, 128), BF),
        in_specs=[VM, VM, VM],
        out_specs=VM,
        compiler_params=params(),
    )(got, radiate, near)


def solution(mesh):
    in_specs = (
        P("clus", None, None),
        P(("clus", "samp"), None, None, None),
        P(("clus", "samp"), None, None, None, None),
        P(("clus", "samp"), None),
        P("clus"),
        P("samp", None),
        P(),
        P("clus", None),
        P("clus", None),
        P("clus", None),
        P(None, None, "samp"),
    )
    out_specs = P(("clus", "samp"), None, None)
    return jax.shard_map(body, mesh=mesh, in_specs=in_specs, out_specs=out_specs, check_vma=False)
```

```python
import jax
import jax.numpy as jnp
from jax import lax
from jax.experimental import pallas as pl
from jax.experimental.pallas import tpu as pltpu
from jax.sharding import PartitionSpec as P

BF = jnp.bfloat16
F32 = jnp.float32
VMEM_LIMIT = 16 * 1024 * 1024
VM = pl.BlockSpec(memory_space=pltpu.VMEM)
SM = pl.BlockSpec(memory_space=pltpu.SMEM)


def nt_dot(a, b):
    return lax.dot_general(a, b, (((1,), (1,)), ((), ())), preferred_element_type=F32)


def nn_dot(a, b):
    return lax.dot_general(a, b, (((1,), (0,)), ((), ())), preferred_element_type=F32)


def tn_dot(a, b):
    return lax.dot_general(a, b, (((0,), (0,)), ((), ())), preferred_element_type=F32)


def rows_of(shape, dim):
    return lax.broadcasted_iota(jnp.int32, shape, dim)


def radiate_kernel(cur, rad_all, itp, tra, out, own, rad, half_ref, tran, sems):
    clus = lax.axis_index("clus")
    mine = pl.ds(pl.multiple_of(lax.rem(clus, 2) * 128, 128), 128)
    pairs = [
        (itp.at[mine], half_ref),
        (tra.at[clus], tran),
        (cur.at[pl.ds(lax.axis_index("samp") * 4, 4)], own),
    ] + [(rad_all.at[c], rad.at[c]) for c in range(4)]
    copies = [pltpu.make_async_copy(a, b, sems.at[i]) for i, (a, b) in enumerate(pairs)]
    for copy in copies:
        copy.start()
    copies[0].wait()
    copies[1].wait()
    half = half_ref[...]
    trow = tran[...].astype(F32)
    row = rows_of((8, 256), 0)
    extra = jnp.where(row == 0, trow[0:1], jnp.where(row == 1, trow[1:2], 0.0)).astype(BF)
    for s in range(8):
        out[s, 64:192, :] = half
        out[s, 192:200, :] = extra
    copies[2].wait()
    for c in range(4):
        copies[3 + c].wait()
        values = own[c].astype(F32).T.astype(BF)
        with_real = nt_dot(values, rad[c, 0])
        with_imag = nt_dot(values, rad[c, 1])
        real = with_real[:64] - with_imag[64:]
        imag = with_real[64:] + with_imag[:64]
        for s in range(8):
            both = jnp.concatenate([real[8 * s : 8 * s + 8], imag[8 * s : 8 * s + 8]], axis=0)
            out[s, 16 * c : 16 * c + 16, :] = both.astype(BF)


def own_lanes(k):
    core = lax.rem(lax.axis_index("clus"), 2)
    return pl.ds(pl.multiple_of(k * 256 + core * 128, 128), 128)


def other_lanes(k):
    core = lax.rem(lax.axis_index("clus"), 2)
    return pl.ds(pl.multiple_of(k * 256 + (1 - core) * 128, 128), 128)


def lift_halves(rows, matrix, cosines, sines):
    reals, imags = ([], []), ([], [])
    for p in range(4):
        lifted = nt_dot(rows[128 * p : 128 * p + 128, :], matrix)
        for h in range(2):
            lanes = slice(128 * h, 128 * h + 128)
            real_sum = imag_sum = None
            for o in range(8):
                re = lifted[16 * o : 16 * o + 8, lanes]
                im = lifted[16 * o + 8 : 16 * o + 16, lanes]
                co, si = cosines[h][o : o + 1], sines[h][o : o + 1]
                real = re * co - im * si
                imag = re * si + im * co
                real_sum = real if real_sum is None else real_sum + real
                imag_sum = imag if imag_sum is None else imag_sum + imag
            reals[h].append(real_sum)
            imags[h].append(imag_sum)
    stacks = [jnp.stack(reals[h] + imags[h], axis=0) for h in range(2)]
    return [jnp.swapaxes(stack, 0, 1).astype(BF) for stack in stacks]


def lift_own_kernel(slots, got, cosine, sine, out, rows, inverse):
    for c in range(32):
        inverse[slots[c]] = c
    for n in range(32):
        c = inverse[n]
        src = pl.multiple_of(lax.rem(c, 4) * 16, 16)
        rows[16 * n : 16 * n + 16, :] = got[lax.div(c, 4), pl.ds(src, 16), :]
    for k in range(0, 8, 2):
        lanes = [own_lanes(k), own_lanes(k + 1)]
        matrix = jnp.concatenate([got[k, 64:192, :], got[k + 1, 64:192, :]], axis=0)
        cosines = [cosine[:, at] for at in lanes]
        sines = [sine[:, at] for at in lanes]
        blocks = lift_halves(rows, matrix, cosines, sines)
        for h in range(2):
            for r in range(8):
                out[r // 2, k + h, r % 2] = blocks[h][r]


def lift_other_kernel(first, rows, got, other, lists, cosine, sine, out):
    row = rows_of((8, 128), 0)
    for k in range(0, 8, 2):
        lanes = [other_lanes(k), other_lanes(k + 1)]
        matrix = jnp.concatenate([other[k], other[k + 1]], axis=0)
        cosines = [cosine[:, at] for at in lanes]
        sines = [sine[:, at] for at in lanes]
        blocks = lift_halves(rows, matrix, cosines, sines)
        for h in range(2):
            tran = got[k + h, 192:200, :].astype(F32)
            tile = lists[...]
            for j in range(4):
                piece = tran[j // 2 : j // 2 + 1, 128 * (j % 2) : 128 * (j % 2) + 128]
                tile = jnp.where(row == 4 + j, piece, tile)
            tile = tile.astype(BF)
            for r in range(8):
                out[r // 2, k + h, r % 2, :, 0:128] = first[r // 2, k + h, r % 2]
                out[r // 2, k + h, r % 2, :, 128:256] = blocks[h][r]
                out[r // 2, k + h, r % 2, :, 256:384] = tile


def translate_kernel(got, out, table, codes, tran, real_acc, imag_acc):
    def uppers(even, odd):
        low = rows_of(even.shape, 1) < 4
        return jnp.where(low, even, pltpu.roll(odd, 4, 1)).reshape(256, even.shape[2])

    def lowers(even, odd):
        low = rows_of(even.shape, 1) < 4
        return jnp.where(low, pltpu.roll(even, 4, 1), odd).reshape(256, even.shape[2])

    for h in range(2):
        even = got[:, 0, :, 128 * h : 128 * h + 128].astype(F32)
        odd = got[:, 1, :, 128 - 128 * h : 256 - 128 * h].astype(F32)
        table[:, 128 * h : 128 * h + 128] = uppers(even, odd).astype(BF)
        table[:, 256 + 128 * h : 384 + 128 * h] = lowers(even, odd).astype(BF)
    even = got[:, 0, :, 256:384].astype(F32)
    odd = got[:, 1, :, 256:384].astype(F32)
    codes[...] = uppers(even, odd).astype(jnp.int32)
    pieces = lowers(even, odd).astype(BF)
    for j in range(4):
        pick = rows_of((64, 256), 1) == rows_of((64, 256), 0) * 4 + j
        part = nn_dot(pick.astype(F32).astype(BF), pieces)
        tran[:, 128 * j : 128 * j + 128] = part.astype(BF)
    col = rows_of((256, 256), 1)
    kinds = rows_of((256, 64), 1)
    for f in range(16):
        pick = (col == codes[:, f : f + 1]).astype(F32).astype(BF)
        kind = (kinds == codes[:, 16 + f : 17 + f]).astype(F32).astype(BF)
        both = nn_dot(pick, table[...])
        factor = nn_dot(kind, tran[...])
        re, im = both[:, :256], both[:, 256:]
        tre, tim = factor[:, :256], factor[:, 256:]
        real = re * tre - im * tim
        imag = re * tim + im * tre
        if f == 0:
            real_acc[...] = real
            imag_acc[...] = imag
        else:
            real_acc[...] += real
            imag_acc[...] += imag
    low = rows_of((32, 8, 256), 1) < 4
    re = real_acc[...].reshape(32, 8, 256)
    im = imag_acc[...].reshape(32, 8, 256)
    out[:, 0] = jnp.where(low, re, pltpu.roll(im, 4, 1)).astype(BF)
    last = jnp.where(low, pltpu.roll(re, 4, 1), im).astype(BF)
    out[:, 1, :, 0:128] = last[:, :, 128:256]
    out[:, 1, :, 128:256] = last[:, :, 0:128]


def descend_kernel(slots, got, half, other, cosine, sine, out, lhs, acc):
    for k in range(8):
        block = jnp.stack([got[r // 2, k, r % 2].astype(F32) for r in range(8)], axis=0)
        block = jnp.swapaxes(block, 0, 1)
        for h, at in enumerate((own_lanes(k), other_lanes(k))):
            lanes = slice(128 * h, 128 * h + 128)
            cos, sin = cosine[:, at], sine[:, at]
            for o in range(8):
                co = jnp.broadcast_to(cos[o : o + 1], (8, 128))
                si = jnp.broadcast_to(sin[o : o + 1], (8, 128))
                for p in range(4):
                    re, im = block[p][:, lanes], block[4 + p][:, lanes]
                    both = jnp.concatenate([re * co + im * si, im * co - re * si], axis=0)
                    n = 8 * p + o
                    lhs[k, 16 * n : 16 * n + 16, lanes] = both.astype(BF)
    for first in range(0, 512, 256):
        total = None
        for k in range(8):
            whole = jnp.concatenate([half[k], other[k]], axis=0)
            part = nn_dot(lhs[k, first : first + 256, :], whole)
            total = part if total is None else total + part
        acc[first : first + 256, :] = total
    for c in range(32):
        src = pl.multiple_of(slots[c] * 16, 16)
        out[c // 4, 16 * (c % 4) : 16 * (c % 4) + 16, :] = acc[pl.ds(src, 16), :].astype(BF)


def finish_kernel(got, rad, near, out):
    for c in range(4):
        pieces = [got[s, 16 * c : 16 * c + 16, :].astype(F32) for s in range(8)]
        rows = jnp.concatenate([q[:8] for q in pieces] + [q[8:] for q in pieces], axis=0)
        received = rows.T.astype(BF)
        with_real = tn_dot(rad[c, 0], received)
        with_imag = tn_dot(rad[c, 1], received)
        turned = pltpu.roll(with_imag, 64, 1)
        lane = rows_of((128, 128), 1)
        far = with_real + jnp.where(lane < 64, turned, -turned)
        out[c] = (near[c] + far).astype(BF)


def params(limit=VMEM_LIMIT):
    return pltpu.CompilerParams(vmem_limit_bytes=limit)


def combine_parts(with_real, with_imag, sign):
    half_width = with_real.shape[-1] // 2
    real_part = with_real[..., :half_width] - sign * with_imag[..., half_width:]
    imag_part = with_real[..., half_width:] + sign * with_imag[..., :half_width]
    return jnp.concatenate([real_part, imag_part], axis=-1)


def near_field(currents, near_blocks, near_cols):
    group = currents.shape[0]
    margin = group // 4
    count = lax.axis_size("clus")
    up = [(i, i + 1) for i in range(count - 1)]
    down = [(b, a) for a, b in up]
    low = lax.ppermute(currents[group - margin :], "clus", up)
    high = lax.ppermute(currents[:margin], "clus", down)
    window = jnp.concatenate([low, currents, high], axis=0)
    local = near_cols - (lax.axis_index("clus") * group - margin)
    neighbours = window[local]
    near_real = jnp.einsum(
        "cjab,cjbr->car", near_blocks[:, :, 0], neighbours, preferred_element_type=F32
    )
    near_imag = jnp.einsum(
        "cjab,cjbr->car", near_blocks[:, :, 1], neighbours, preferred_element_type=F32
    )
    return combine_parts(near_real, near_imag, 1.0)


def body(
    currents,
    radiate,
    near_blocks,
    near_cols,
    child_slot,
    interp,
    shift_angle,
    far_dev,
    far_loc,
    far_type,
    transl,
):
    partner = [(i, i ^ 1) for i in range(lax.axis_size("clus"))]
    exchange = lambda x, axis: lax.all_to_all(x, axis, split_axis=0, concat_axis=0, tiled=True)
    lists = jnp.pad((far_dev * 4 + far_loc).astype(F32), ((0, 4), (0, 112)))
    lists = lists + jnp.pad(far_type.astype(F32), ((0, 4), (16, 96)))
    cosine = jnp.cos(shift_angle)
    sine = jnp.sin(shift_angle)

    sent = pl.pallas_call(
        radiate_kernel,
        name="radiate",
        out_shape=jax.ShapeDtypeStruct((8, 200, 256), BF),
        in_specs=[pl.BlockSpec(memory_space=pltpu.HBM)] * 4,
        out_specs=VM,
        scratch_shapes=[
            pltpu.VMEM((4, 128, 128), BF),
            pltpu.VMEM((4, 2, 256, 128), BF),
            pltpu.VMEM((128, 256), BF),
            pltpu.VMEM((2, 256), BF),
            pltpu.SemaphoreType.DMA((7,)),
        ],
        compiler_params=params(60 * 1024 * 1024),
    )(currents, radiate, interp, transl)
    got = exchange(sent, "samp")
    half = got[:, 64:192]
    other = lax.ppermute(half, "clus", partner)

    first, rows = pl.pallas_call(
        lift_own_kernel,
        name="lift_own",
        out_shape=(
            jax.ShapeDtypeStruct((4, 8, 2, 8, 128), BF),
            jax.ShapeDtypeStruct((512, 256), BF),
        ),
        in_specs=[SM, VM, VM, VM],
        out_specs=(VM, VM),
        scratch_shapes=[pltpu.SMEM((32,), jnp.int32)],
        compiler_params=params(),
    )(child_slot, got, cosine, sine)
    sent = pl.pallas_call(
        lift_other_kernel,
        name="lift_other",
        out_shape=jax.ShapeDtypeStruct((4, 8, 2, 8, 384), BF),
        in_specs=[VM] * 7,
        out_specs=VM,
        compiler_params=params(),
    )(first, rows, got, other, lists, cosine, sine)
    moved = exchange(sent.reshape(64, 8, 384), "clus")

    sent = pl.pallas_call(
        translate_kernel,
        name="translate",
        out_shape=jax.ShapeDtypeStruct((32, 2, 8, 256), BF),
        in_specs=[VM],
        out_specs=VM,
        scratch_shapes=[
            pltpu.VMEM((256, 512), BF),
            pltpu.VMEM((256, 128), jnp.int32),
            pltpu.VMEM((64, 512), BF),
            pltpu.VMEM((256, 256), F32),
            pltpu.VMEM((256, 256), F32),
        ],
        compiler_params=params(),
    )(moved.reshape(32, 2, 8, 384))
    moved = exchange(sent.reshape(64, 8, 256), "clus")

    sent = pl.pallas_call(
        descend_kernel,
        name="descend",
        out_shape=jax.ShapeDtypeStruct((8, 64, 256), BF),
        in_specs=[SM, VM, VM, VM, VM, VM],
        out_specs=VM,
        scratch_shapes=[
            pltpu.VMEM((8, 512, 256), BF),
            pltpu.VMEM((512, 256), F32),
        ],
        compiler_params=params(),
    )(child_slot, moved.reshape(4, 8, 2, 8, 256), half, other, cosine, sine)
    got = exchange(sent, "samp")

    near = near_field(currents, near_blocks, near_cols)
    return pl.pallas_call(
        finish_kernel,
        name="finish",
        out_shape=jax.ShapeDtypeStruct((4, 128, 128), BF),
        in_specs=[VM, VM, VM],
        out_specs=VM,
        compiler_params=params(),
    )(got, radiate, near)


def solution(mesh):
    in_specs = (
        P("clus", None, None),
        P(("clus", "samp"), None, None, None),
        P(("clus", "samp"), None, None, None, None),
        P(("clus", "samp"), None),
        P("clus"),
        P("samp", None),
        P(),
        P("clus", None),
        P("clus", None),
        P("clus", None),
        P(None, None, "samp"),
    )
    out_specs = P(("clus", "samp"), None, None)
    return jax.shard_map(body, mesh=mesh, in_specs=in_specs, out_specs=out_specs, check_vma=False)
```

```python
import jax
import jax.numpy as jnp
from jax import lax
from jax.experimental import pallas as pl
from jax.experimental.pallas import tpu as pltpu
from jax.sharding import PartitionSpec as P

BF = jnp.bfloat16
F32 = jnp.float32
VMEM_LIMIT = 16 * 1024 * 1024
VM = pl.BlockSpec(memory_space=pltpu.VMEM)
SM = pl.BlockSpec(memory_space=pltpu.SMEM)


def nt_dot(a, b):
    return lax.dot_general(a, b, (((1,), (1,)), ((), ())), preferred_element_type=F32)


def nn_dot(a, b):
    return lax.dot_general(a, b, (((1,), (0,)), ((), ())), preferred_element_type=F32)


def tn_dot(a, b):
    return lax.dot_general(a, b, (((0,), (0,)), ((), ())), preferred_element_type=F32)


def rows_of(shape, dim):
    return lax.broadcasted_iota(jnp.int32, shape, dim)


def radiate_kernel(
    cur, rad_all, itp, tra, out, own, rad, half, tran, data, extra, in_sems, out_sems
):
    clus = lax.axis_index("clus")
    mine = pl.ds(pl.multiple_of(lax.rem(clus, 2) * 128, 128), 128)
    pairs = [
        (itp.at[mine], half),
        (tra.at[clus], tran),
        (cur.at[pl.ds(lax.axis_index("samp") * 4, 4)], own),
    ] + [(rad_all.at[c], rad.at[c]) for c in range(4)]
    copies = [pltpu.make_async_copy(a, b, in_sems.at[i]) for i, (a, b) in enumerate(pairs)]
    for copy in copies:
        copy.start()
    copies[0].wait()
    copies[1].wait()
    trow = tran[...].astype(F32)
    row = rows_of((8, 256), 0)
    extra[...] = jnp.where(row == 0, trow[0:1], jnp.where(row == 1, trow[1:2], 0.0)).astype(BF)
    sends = []
    for s in range(8):
        sends.append(pltpu.make_async_copy(half, out.at[s, 64:192, :], out_sems.at[s]))
        sends.append(pltpu.make_async_copy(extra, out.at[s, 192:200, :], out_sems.at[8 + s]))
    for send in sends:
        send.start()
    copies[2].wait()
    for c in range(4):
        copies[3 + c].wait()
        values = own[c].astype(F32).T.astype(BF)
        with_real = nt_dot(values, rad[c, 0])
        with_imag = nt_dot(values, rad[c, 1])
        real = with_real[:64] - with_imag[64:]
        imag = with_real[64:] + with_imag[:64]
        for s in range(8):
            both = jnp.concatenate([real[8 * s : 8 * s + 8], imag[8 * s : 8 * s + 8]], axis=0)
            data[s, 16 * c : 16 * c + 16, :] = both.astype(BF)
    last = pltpu.make_async_copy(data, out.at[:, 0:64, :], out_sems.at[16])
    last.start()
    for send in sends:
        send.wait()
    last.wait()


def own_lanes(k):
    core = lax.rem(lax.axis_index("clus"), 2)
    return pl.ds(pl.multiple_of(k * 256 + core * 128, 128), 128)


def other_lanes(k):
    core = lax.rem(lax.axis_index("clus"), 2)
    return pl.ds(pl.multiple_of(k * 256 + (1 - core) * 128, 128), 128)


def lift_halves(rows, matrix, cosines, sines):
    reals, imags = ([], []), ([], [])
    for p in range(4):
        lifted = nt_dot(rows[128 * p : 128 * p + 128, :], matrix)
        for h in range(2):
            lanes = slice(128 * h, 128 * h + 128)
            real_sum = imag_sum = None
            for o in range(8):
                re = lifted[16 * o : 16 * o + 8, lanes]
                im = lifted[16 * o + 8 : 16 * o + 16, lanes]
                co, si = cosines[h][o : o + 1], sines[h][o : o + 1]
                real = re * co - im * si
                imag = re * si + im * co
                real_sum = real if real_sum is None else real_sum + real
                imag_sum = imag if imag_sum is None else imag_sum + imag
            reals[h].append(real_sum)
            imags[h].append(imag_sum)
    stacks = [jnp.stack(reals[h] + imags[h], axis=0) for h in range(2)]
    return [jnp.swapaxes(stack, 0, 1).astype(BF) for stack in stacks]


def lift_own_kernel(slots, got, cosine, sine, out, rows, inverse):
    for c in range(32):
        inverse[slots[c]] = c
    for n in range(32):
        c = inverse[n]
        src = pl.multiple_of(lax.rem(c, 4) * 16, 16)
        rows[16 * n : 16 * n + 16, :] = got[lax.div(c, 4), pl.ds(src, 16), :]
    for k in range(0, 8, 2):
        lanes = [own_lanes(k), own_lanes(k + 1)]
        matrix = jnp.concatenate([got[k, 64:192, :], got[k + 1, 64:192, :]], axis=0)
        cosines = [cosine[:, at] for at in lanes]
        sines = [sine[:, at] for at in lanes]
        blocks = lift_halves(rows, matrix, cosines, sines)
        for h in range(2):
            for r in range(8):
                out[r // 2, k + h, r % 2] = blocks[h][r]


def lift_other_kernel(first, rows, got, other, lists, cosine, sine, out):
    row = rows_of((8, 128), 0)
    for k in range(0, 8, 2):
        lanes = [other_lanes(k), other_lanes(k + 1)]
        matrix = jnp.concatenate([other[k], other[k + 1]], axis=0)
        cosines = [cosine[:, at] for at in lanes]
        sines = [sine[:, at] for at in lanes]
        blocks = lift_halves(rows, matrix, cosines, sines)
        for h in range(2):
            tran = got[k + h, 192:200, :].astype(F32)
            tile = lists[...]
            for j in range(4):
                piece = tran[j // 2 : j // 2 + 1, 128 * (j % 2) : 128 * (j % 2) + 128]
                tile = jnp.where(row == 4 + j, piece, tile)
            tile = tile.astype(BF)
            for r in range(8):
                out[r // 2, k + h, r % 2, :, 0:128] = first[r // 2, k + h, r % 2]
                out[r // 2, k + h, r % 2, :, 128:256] = blocks[h][r]
                out[r // 2, k + h, r % 2, :, 256:384] = tile


def translate_kernel(got, out, table, codes, tran, real_acc, imag_acc):
    def uppers(even, odd):
        low = rows_of(even.shape, 1) < 4
        return jnp.where(low, even, pltpu.roll(odd, 4, 1)).reshape(256, even.shape[2])

    def lowers(even, odd):
        low = rows_of(even.shape, 1) < 4
        return jnp.where(low, pltpu.roll(even, 4, 1), odd).reshape(256, even.shape[2])

    for h in range(2):
        even = got[:, 0, :, 128 * h : 128 * h + 128].astype(F32)
        odd = got[:, 1, :, 128 - 128 * h : 256 - 128 * h].astype(F32)
        table[:, 128 * h : 128 * h + 128] = uppers(even, odd).astype(BF)
        table[:, 256 + 128 * h : 384 + 128 * h] = lowers(even, odd).astype(BF)
    even = got[:, 0, :, 256:384].astype(F32)
    odd = got[:, 1, :, 256:384].astype(F32)
    codes[...] = uppers(even, odd).astype(jnp.int32)
    pieces = lowers(even, odd).astype(BF)
    for j in range(4):
        pick = rows_of((128, 256), 1) == rows_of((128, 256), 0) * 4 + j
        part = nn_dot(pick.astype(F32).astype(BF), pieces)
        tran[:, 128 * j : 128 * j + 128] = part.astype(BF)
    col = rows_of((256, 256), 1)
    kinds = rows_of((256, 128), 1)
    for first in range(0, 16, 4):
        picks = [(col == codes[:, first + f : first + f + 1]).astype(F32) for f in range(4)]
        turns = [(kinds == codes[:, 16 + first + f : 17 + first + f]).astype(F32) for f in range(4)]
        both = nn_dot(jnp.concatenate([p.astype(BF) for p in picks], axis=0), table[...])
        factor = nn_dot(jnp.concatenate([t.astype(BF) for t in turns], axis=0), tran[...])
        real = imag = None
        for f in range(4):
            rows = slice(256 * f, 256 * f + 256)
            re, im = both[rows, :256], both[rows, 256:]
            tre, tim = factor[rows, :256], factor[rows, 256:]
            add_real = re * tre - im * tim
            add_imag = re * tim + im * tre
            real = add_real if real is None else real + add_real
            imag = add_imag if imag is None else imag + add_imag
        if first == 0:
            real_acc[...] = real
            imag_acc[...] = imag
        else:
            real_acc[...] += real
            imag_acc[...] += imag
    low = rows_of((32, 8, 256), 1) < 4
    re = real_acc[...].reshape(32, 8, 256)
    im = imag_acc[...].reshape(32, 8, 256)
    out[:, 0] = jnp.where(low, re, pltpu.roll(im, 4, 1)).astype(BF)
    last = jnp.where(low, pltpu.roll(re, 4, 1), im).astype(BF)
    out[:, 1, :, 0:128] = last[:, :, 128:256]
    out[:, 1, :, 128:256] = last[:, :, 0:128]


def descend_kernel(slots, got, half, other, cosine, sine, out, lhs, acc):
    for k in range(8):
        block = jnp.stack([got[r // 2, k, r % 2].astype(F32) for r in range(8)], axis=0)
        block = jnp.swapaxes(block, 0, 1)
        for h, at in enumerate((own_lanes(k), other_lanes(k))):
            lanes = slice(128 * h, 128 * h + 128)
            cos, sin = cosine[:, at], sine[:, at]
            for o in range(8):
                co = jnp.broadcast_to(cos[o : o + 1], (8, 128))
                si = jnp.broadcast_to(sin[o : o + 1], (8, 128))
                for p in range(4):
                    re, im = block[p][:, lanes], block[4 + p][:, lanes]
                    both = jnp.concatenate([re * co + im * si, im * co - re * si], axis=0)
                    n = 8 * p + o
                    lhs[k, 16 * n : 16 * n + 16, lanes] = both.astype(BF)
    for first in range(0, 512, 256):
        total = None
        for k in range(8):
            whole = jnp.concatenate([half[k], other[k]], axis=0)
            part = nn_dot(lhs[k, first : first + 256, :], whole)
            total = part if total is None else total + part
        acc[first : first + 256, :] = total
    for c in range(32):
        src = pl.multiple_of(slots[c] * 16, 16)
        out[c // 4, 16 * (c % 4) : 16 * (c % 4) + 16, :] = acc[pl.ds(src, 16), :].astype(BF)


def finish_kernel(got, rad, near, out):
    for c in range(4):
        pieces = [got[s, 16 * c : 16 * c + 16, :].astype(F32) for s in range(8)]
        rows = jnp.concatenate([q[:8] for q in pieces] + [q[8:] for q in pieces], axis=0)
        received = rows.T.astype(BF)
        with_real = tn_dot(rad[c, 0], received)
        with_imag = tn_dot(rad[c, 1], received)
        turned = pltpu.roll(with_imag, 64, 1)
        lane = rows_of((128, 128), 1)
        far = with_real + jnp.where(lane < 64, turned, -turned)
        out[c] = (near[c] + far).astype(BF)


def params(limit=VMEM_LIMIT):
    return pltpu.CompilerParams(vmem_limit_bytes=limit)


def near_kernel(cols, low, cur, high, blocks, out, window, sems):
    pairs = [(low, window.at[0:8]), (cur, window.at[8:40]), (high, window.at[40:48])]
    copies = [pltpu.make_async_copy(a, b, sems.at[i]) for i, (a, b) in enumerate(pairs)]
    for copy in copies:
        copy.start()
    for copy in copies:
        copy.wait()
    start = lax.axis_index("clus") * 32 - 8

    def row(c, carry):
        total = None
        for j in range(10):
            part = nn_dot(blocks[c, j].reshape(256, 128), window[cols[c, j] - start])
            total = part if total is None else total + part
        turned = pltpu.roll(total[128:], 64, 1)
        lane = rows_of((128, 128), 1)
        out[c] = total[:128] + jnp.where(lane < 64, -turned, turned)
        return carry

    lax.fori_loop(0, 4, row, 0)


def halo(currents):
    up = [(i, i + 1) for i in range(lax.axis_size("clus") - 1)]
    down = [(b, a) for a, b in up]
    return lax.ppermute(currents[24:32], "clus", up), lax.ppermute(currents[0:8], "clus", down)


def near_field(currents, low, high, near_blocks, near_cols):
    hbm = pl.BlockSpec(memory_space=pltpu.HBM)
    return pl.pallas_call(
        near_kernel,
        name="near",
        out_shape=jax.ShapeDtypeStruct((4, 128, 128), F32),
        in_specs=[SM, hbm, hbm, hbm, VM],
        out_specs=VM,
        scratch_shapes=[pltpu.VMEM((48, 128, 128), BF), pltpu.SemaphoreType.DMA((3,))],
        cost_estimate=pl.CostEstimate(flops=168000000, bytes_accessed=4600000, transcendentals=0),
        compiler_params=params(),
    )(near_cols, low, currents, high, near_blocks)


def body(
    currents,
    radiate,
    near_blocks,
    near_cols,
    child_slot,
    interp,
    shift_angle,
    far_dev,
    far_loc,
    far_type,
    transl,
):
    partner = [(i, i ^ 1) for i in range(lax.axis_size("clus"))]
    exchange = lambda x, axis: lax.all_to_all(x, axis, split_axis=0, concat_axis=0, tiled=True)
    lists = jnp.pad((far_dev * 4 + far_loc).astype(F32), ((0, 4), (0, 112)))
    lists = lists + jnp.pad(far_type.astype(F32), ((0, 4), (16, 96)))
    cosine = jnp.cos(shift_angle)
    sine = jnp.sin(shift_angle)

    sent = pl.pallas_call(
        radiate_kernel,
        name="radiate",
        out_shape=jax.ShapeDtypeStruct((8, 200, 256), BF),
        in_specs=[pl.BlockSpec(memory_space=pltpu.HBM)] * 4,
        out_specs=pl.BlockSpec(memory_space=pltpu.HBM),
        scratch_shapes=[
            pltpu.VMEM((4, 128, 128), BF),
            pltpu.VMEM((4, 2, 256, 128), BF),
            pltpu.VMEM((128, 256), BF),
            pltpu.VMEM((2, 256), BF),
            pltpu.VMEM((8, 64, 256), BF),
            pltpu.VMEM((8, 256), BF),
            pltpu.SemaphoreType.DMA((7,)),
            pltpu.SemaphoreType.DMA((17,)),
        ],
        compiler_params=params(60 * 1024 * 1024),
    )(currents, radiate, interp, transl)
    got = exchange(sent, "samp")
    half = got[:, 64:192]
    other = lax.ppermute(half, "clus", partner)

    first, rows = pl.pallas_call(
        lift_own_kernel,
        name="lift_own",
        out_shape=(
            jax.ShapeDtypeStruct((4, 8, 2, 8, 128), BF),
            jax.ShapeDtypeStruct((512, 256), BF),
        ),
        in_specs=[SM, VM, VM, VM],
        out_specs=(VM, VM),
        scratch_shapes=[pltpu.SMEM((32,), jnp.int32)],
        compiler_params=params(),
    )(child_slot, got, cosine, sine)
    sent = pl.pallas_call(
        lift_other_kernel,
        name="lift_other",
        out_shape=jax.ShapeDtypeStruct((4, 8, 2, 8, 384), BF),
        in_specs=[VM] * 7,
        out_specs=VM,
        compiler_params=params(),
    )(first, rows, got, other, lists, cosine, sine)
    moved = exchange(sent.reshape(64, 8, 384), "clus")
    low, high = halo(currents)
    moved, low, high = lax.optimization_barrier((moved, low, high))

    sent = pl.pallas_call(
        translate_kernel,
        name="translate",
        out_shape=jax.ShapeDtypeStruct((32, 2, 8, 256), BF),
        in_specs=[VM],
        out_specs=VM,
        scratch_shapes=[
            pltpu.VMEM((256, 512), BF),
            pltpu.VMEM((256, 128), jnp.int32),
            pltpu.VMEM((128, 512), BF),
            pltpu.VMEM((256, 256), F32),
            pltpu.VMEM((256, 256), F32),
        ],
        compiler_params=params(),
    )(moved.reshape(32, 2, 8, 384))
    moved = exchange(sent.reshape(64, 8, 256), "clus")
    near = near_field(currents, low, high, near_blocks, near_cols)
    moved, near = lax.optimization_barrier((moved, near))

    sent = pl.pallas_call(
        descend_kernel,
        name="descend",
        out_shape=jax.ShapeDtypeStruct((8, 64, 256), BF),
        in_specs=[SM, VM, VM, VM, VM, VM],
        out_specs=VM,
        scratch_shapes=[
            pltpu.VMEM((8, 512, 256), BF),
            pltpu.VMEM((512, 256), F32),
        ],
        compiler_params=params(),
    )(child_slot, moved.reshape(4, 8, 2, 8, 256), half, other, cosine, sine)
    got = exchange(sent, "samp")

    return pl.pallas_call(
        finish_kernel,
        name="finish",
        out_shape=jax.ShapeDtypeStruct((4, 128, 128), BF),
        in_specs=[VM, VM, VM],
        out_specs=VM,
        compiler_params=params(),
    )(got, radiate, near)


def solution(mesh):
    in_specs = (
        P("clus", None, None),
        P(("clus", "samp"), None, None, None),
        P(("clus", "samp"), None, None, None, None),
        P(("clus", "samp"), None),
        P("clus"),
        P("samp", None),
        P(),
        P("clus", None),
        P("clus", None),
        P("clus", None),
        P(None, None, "samp"),
    )
    out_specs = P(("clus", "samp"), None, None)
    return jax.shard_map(body, mesh=mesh, in_specs=in_specs, out_specs=out_specs, check_vma=False)
```

```python
import jax
import jax.numpy as jnp
from jax import lax
from jax.experimental import pallas as pl
from jax.experimental.pallas import tpu as pltpu
from jax.sharding import PartitionSpec as P

BF = jnp.bfloat16
F32 = jnp.float32
VMEM_LIMIT = 16 * 1024 * 1024
VM = pl.BlockSpec(memory_space=pltpu.VMEM)
SM = pl.BlockSpec(memory_space=pltpu.SMEM)


def nt_dot(a, b):
    return lax.dot_general(a, b, (((1,), (1,)), ((), ())), preferred_element_type=F32)


def nn_dot(a, b):
    return lax.dot_general(a, b, (((1,), (0,)), ((), ())), preferred_element_type=F32)


def tn_dot(a, b):
    return lax.dot_general(a, b, (((0,), (0,)), ((), ())), preferred_element_type=F32)


def rows_of(shape, dim):
    return lax.broadcasted_iota(jnp.int32, shape, dim)


def radiate_kernel(
    cur, rad_all, itp, tra, out, own, rad, half, tran, data, extra, in_sems, out_sems
):
    clus = lax.axis_index("clus")
    mine = pl.ds(pl.multiple_of(lax.rem(clus, 2) * 128, 128), 128)
    pairs = [
        (itp.at[mine], half),
        (tra.at[clus], tran),
        (cur.at[pl.ds(lax.axis_index("samp") * 4, 4)], own),
    ] + [(rad_all.at[c], rad.at[c]) for c in range(4)]
    copies = [pltpu.make_async_copy(a, b, in_sems.at[i]) for i, (a, b) in enumerate(pairs)]
    for copy in copies:
        copy.start()
    copies[0].wait()
    copies[1].wait()
    trow = tran[...].astype(F32)
    row = rows_of((8, 256), 0)
    extra[...] = jnp.where(row == 0, trow[0:1], jnp.where(row == 1, trow[1:2], 0.0)).astype(BF)
    sends = []
    for s in range(8):
        sends.append(pltpu.make_async_copy(half, out.at[s, 64:192, :], out_sems.at[s]))
        sends.append(pltpu.make_async_copy(extra, out.at[s, 192:200, :], out_sems.at[8 + s]))
    for send in sends:
        send.start()
    copies[2].wait()
    for c in range(4):
        copies[3 + c].wait()
        values = own[c].astype(F32).T.astype(BF)
        with_real = nt_dot(values, rad[c, 0])
        with_imag = nt_dot(values, rad[c, 1])
        real = with_real[:64] - with_imag[64:]
        imag = with_real[64:] + with_imag[:64]
        for s in range(8):
            both = jnp.concatenate([real[8 * s : 8 * s + 8], imag[8 * s : 8 * s + 8]], axis=0)
            data[s, 16 * c : 16 * c + 16, :] = both.astype(BF)
    last = pltpu.make_async_copy(data, out.at[:, 0:64, :], out_sems.at[16])
    last.start()
    for send in sends:
        send.wait()
    last.wait()


def own_lanes(k):
    core = lax.rem(lax.axis_index("clus"), 2)
    return pl.ds(pl.multiple_of(k * 256 + core * 128, 128), 128)


def other_lanes(k):
    core = lax.rem(lax.axis_index("clus"), 2)
    return pl.ds(pl.multiple_of(k * 256 + (1 - core) * 128, 128), 128)


def lift_halves(rows, matrix, cosines, sines):
    reals, imags = ([], []), ([], [])
    for p in range(4):
        lifted = nt_dot(rows[128 * p : 128 * p + 128, :], matrix)
        for h in range(2):
            lanes = slice(128 * h, 128 * h + 128)
            real_sum = imag_sum = None
            for o in range(8):
                re = lifted[16 * o : 16 * o + 8, lanes]
                im = lifted[16 * o + 8 : 16 * o + 16, lanes]
                co, si = cosines[h][o : o + 1], sines[h][o : o + 1]
                real = re * co - im * si
                imag = re * si + im * co
                real_sum = real if real_sum is None else real_sum + real
                imag_sum = imag if imag_sum is None else imag_sum + imag
            reals[h].append(real_sum)
            imags[h].append(imag_sum)
    stacks = [jnp.stack(reals[h] + imags[h], axis=0) for h in range(2)]
    return [jnp.swapaxes(stack, 0, 1).astype(BF) for stack in stacks]


def lift_own_kernel(slots, got, cosine, sine, out, rows, inverse):
    for c in range(32):
        inverse[slots[c]] = c
    for n in range(32):
        c = inverse[n]
        src = pl.multiple_of(lax.rem(c, 4) * 16, 16)
        rows[16 * n : 16 * n + 16, :] = got[lax.div(c, 4), pl.ds(src, 16), :]
    for k in range(0, 8, 2):
        lanes = [own_lanes(k), own_lanes(k + 1)]
        matrix = jnp.concatenate([got[k, 64:192, :], got[k + 1, 64:192, :]], axis=0)
        cosines = [cosine[:, at] for at in lanes]
        sines = [sine[:, at] for at in lanes]
        blocks = lift_halves(rows, matrix, cosines, sines)
        for h in range(2):
            for r in range(8):
                out[r // 2, k + h, r % 2] = blocks[h][r]


def lift_other_kernel(first, rows, got, other, lists, cosine, sine, out):
    row = rows_of((8, 128), 0)
    for k in range(0, 8, 2):
        lanes = [other_lanes(k), other_lanes(k + 1)]
        matrix = jnp.concatenate([other[k], other[k + 1]], axis=0)
        cosines = [cosine[:, at] for at in lanes]
        sines = [sine[:, at] for at in lanes]
        blocks = lift_halves(rows, matrix, cosines, sines)
        for h in range(2):
            tran = got[k + h, 192:200, :].astype(F32)
            tile = lists[...]
            for j in range(4):
                piece = tran[j // 2 : j // 2 + 1, 128 * (j % 2) : 128 * (j % 2) + 128]
                tile = jnp.where(row == 4 + j, piece, tile)
            tile = tile.astype(BF)
            for r in range(8):
                out[r // 2, k + h, r % 2, :, 0:128] = first[r // 2, k + h, r % 2]
                out[r // 2, k + h, r % 2, :, 128:256] = blocks[h][r]
                out[r // 2, k + h, r % 2, :, 256:384] = tile


def translate_kernel(got, out, table, codes, tran, real_acc, imag_acc):
    def uppers(even, odd):
        low = rows_of(even.shape, 1) < 4
        return jnp.where(low, even, pltpu.roll(odd, 4, 1)).reshape(256, even.shape[2])

    def lowers(even, odd):
        low = rows_of(even.shape, 1) < 4
        return jnp.where(low, pltpu.roll(even, 4, 1), odd).reshape(256, even.shape[2])

    for h in range(2):
        even = got[:, 0, :, 128 * h : 128 * h + 128].astype(F32)
        odd = got[:, 1, :, 128 - 128 * h : 256 - 128 * h].astype(F32)
        table[:, 128 * h : 128 * h + 128] = uppers(even, odd).astype(BF)
        table[:, 256 + 128 * h : 384 + 128 * h] = lowers(even, odd).astype(BF)
    even = got[:, 0, :, 256:384].astype(F32)
    odd = got[:, 1, :, 256:384].astype(F32)
    codes[...] = uppers(even, odd).astype(jnp.int32)
    pieces = lowers(even, odd).astype(BF)
    for j in range(4):
        pick = rows_of((128, 256), 1) == rows_of((128, 256), 0) * 4 + j
        part = nn_dot(pick.astype(F32).astype(BF), pieces)
        tran[:, 128 * j : 128 * j + 128] = part.astype(BF)
    col = rows_of((256, 256), 1)
    kinds = rows_of((256, 128), 1)
    for first in range(0, 16, 4):
        picks = [(col == codes[:, first + f : first + f + 1]).astype(F32) for f in range(4)]
        turns = [(kinds == codes[:, 16 + first + f : 17 + first + f]).astype(F32) for f in range(4)]
        both = nn_dot(jnp.concatenate([p.astype(BF) for p in picks], axis=0), table[...])
        factor = nn_dot(jnp.concatenate([t.astype(BF) for t in turns], axis=0), tran[...])
        real = imag = None
        for f in range(4):
            rows = slice(256 * f, 256 * f + 256)
            re, im = both[rows, :256], both[rows, 256:]
            tre, tim = factor[rows, :256], factor[rows, 256:]
            add_real = re * tre - im * tim
            add_imag = re * tim + im * tre
            real = add_real if real is None else real + add_real
            imag = add_imag if imag is None else imag + add_imag
        if first == 0:
            real_acc[...] = real
            imag_acc[...] = imag
        else:
            real_acc[...] += real
            imag_acc[...] += imag
    low = rows_of((32, 8, 256), 1) < 4
    re = real_acc[...].reshape(32, 8, 256)
    im = imag_acc[...].reshape(32, 8, 256)
    out[:, 0] = jnp.where(low, re, pltpu.roll(im, 4, 1)).astype(BF)
    last = jnp.where(low, pltpu.roll(re, 4, 1), im).astype(BF)
    out[:, 1, :, 0:128] = last[:, :, 128:256]
    out[:, 1, :, 128:256] = last[:, :, 0:128]


def descend_kernel(slots, got, half, other, cosine, sine, out, lhs, acc):
    for k in range(8):
        block = jnp.stack([got[r // 2, k, r % 2].astype(F32) for r in range(8)], axis=0)
        block = jnp.swapaxes(block, 0, 1)
        for h, at in enumerate((own_lanes(k), other_lanes(k))):
            lanes = slice(128 * h, 128 * h + 128)
            cos, sin = cosine[:, at], sine[:, at]
            for o in range(8):
                co = jnp.broadcast_to(cos[o : o + 1], (8, 128))
                si = jnp.broadcast_to(sin[o : o + 1], (8, 128))
                for p in range(4):
                    re, im = block[p][:, lanes], block[4 + p][:, lanes]
                    both = jnp.concatenate([re * co + im * si, im * co - re * si], axis=0)
                    n = 8 * p + o
                    lhs[k, 16 * n : 16 * n + 16, lanes] = both.astype(BF)
    for first in range(0, 512, 256):
        total = None
        for k in range(8):
            whole = jnp.concatenate([half[k], other[k]], axis=0)
            part = nn_dot(lhs[k, first : first + 256, :], whole)
            total = part if total is None else total + part
        acc[first : first + 256, :] = total
    for c in range(32):
        src = pl.multiple_of(slots[c] * 16, 16)
        out[c // 4, 16 * (c % 4) : 16 * (c % 4) + 16, :] = acc[pl.ds(src, 16), :].astype(BF)


def finish_kernel(got, rad, near, out):
    for c in range(4):
        pieces = [got[s, 16 * c : 16 * c + 16, :].astype(F32) for s in range(8)]
        rows = jnp.concatenate([q[:8] for q in pieces] + [q[8:] for q in pieces], axis=0)
        received = rows.T.astype(BF)
        with_real = tn_dot(rad[c, 0], received)
        with_imag = tn_dot(rad[c, 1], received)
        turned = pltpu.roll(with_imag, 64, 1)
        lane = rows_of((128, 128), 1)
        far = with_real + jnp.where(lane < 64, turned, -turned)
        out[c] = (near[c] + far).astype(BF)


def params(limit=VMEM_LIMIT):
    return pltpu.CompilerParams(vmem_limit_bytes=limit)


def near_kernel(cols, low, cur, high, blocks, out, window, sems):
    pairs = [(low, window.at[0:8]), (cur, window.at[8:40]), (high, window.at[40:48])]
    copies = [pltpu.make_async_copy(a, b, sems.at[i]) for i, (a, b) in enumerate(pairs)]
    for copy in copies:
        copy.start()
    for copy in copies:
        copy.wait()
    start = lax.axis_index("clus") * 32 - 8

    def row(c, carry):
        total = None
        for j in range(10):
            part = nn_dot(blocks[c, j].reshape(256, 128), window[cols[c, j] - start])
            total = part if total is None else total + part
        turned = pltpu.roll(total[128:], 64, 1)
        lane = rows_of((128, 128), 1)
        out[c] = total[:128] + jnp.where(lane < 64, -turned, turned)
        return carry

    lax.fori_loop(0, 4, row, 0)


def halo(currents):
    up = [(i, i + 1) for i in range(lax.axis_size("clus") - 1)]
    down = [(b, a) for a, b in up]
    return lax.ppermute(currents[24:32], "clus", up), lax.ppermute(currents[0:8], "clus", down)


def near_field(currents, low, high, near_blocks, near_cols):
    hbm = pl.BlockSpec(memory_space=pltpu.HBM)
    return pl.pallas_call(
        near_kernel,
        name="near",
        out_shape=jax.ShapeDtypeStruct((4, 128, 128), F32),
        in_specs=[SM, hbm, hbm, hbm, VM],
        out_specs=VM,
        scratch_shapes=[pltpu.VMEM((48, 128, 128), BF), pltpu.SemaphoreType.DMA((3,))],
        cost_estimate=pl.CostEstimate(flops=168000000, bytes_accessed=4600000, transcendentals=0),
        compiler_params=params(),
    )(near_cols, low, currents, high, near_blocks)


def body(
    currents,
    radiate,
    near_blocks,
    near_cols,
    child_slot,
    interp,
    shift_angle,
    far_dev,
    far_loc,
    far_type,
    transl,
):
    partner = [(i, i ^ 1) for i in range(lax.axis_size("clus"))]
    exchange = lambda x, axis: lax.all_to_all(x, axis, split_axis=0, concat_axis=0, tiled=True)
    lists = jnp.pad((far_dev * 4 + far_loc).astype(F32), ((0, 4), (0, 112)))
    lists = lists + jnp.pad(far_type.astype(F32), ((0, 4), (16, 96)))
    cosine = jnp.cos(shift_angle)
    sine = jnp.sin(shift_angle)

    sent = pl.pallas_call(
        radiate_kernel,
        name="radiate",
        out_shape=jax.ShapeDtypeStruct((8, 200, 256), BF),
        in_specs=[pl.BlockSpec(memory_space=pltpu.HBM)] * 4,
        out_specs=pl.BlockSpec(memory_space=pltpu.HBM),
        scratch_shapes=[
            pltpu.VMEM((4, 128, 128), BF),
            pltpu.VMEM((4, 2, 256, 128), BF),
            pltpu.VMEM((128, 256), BF),
            pltpu.VMEM((2, 256), BF),
            pltpu.VMEM((8, 64, 256), BF),
            pltpu.VMEM((8, 256), BF),
            pltpu.SemaphoreType.DMA((7,)),
            pltpu.SemaphoreType.DMA((17,)),
        ],
        compiler_params=params(60 * 1024 * 1024),
    )(currents, radiate, interp, transl)
    sent, mine = lax.optimization_barrier((sent, currents))
    got = exchange(sent, "samp")
    low, high = halo(mine)
    near = near_field(mine, low, high, near_blocks, near_cols)
    got, near = lax.optimization_barrier((got, near))
    half = got[:, 64:192]
    other = lax.ppermute(half, "clus", partner)

    first, rows = pl.pallas_call(
        lift_own_kernel,
        name="lift_own",
        out_shape=(
            jax.ShapeDtypeStruct((4, 8, 2, 8, 128), BF),
            jax.ShapeDtypeStruct((512, 256), BF),
        ),
        in_specs=[SM, VM, VM, VM],
        out_specs=(VM, VM),
        scratch_shapes=[pltpu.SMEM((32,), jnp.int32)],
        compiler_params=params(),
    )(child_slot, got, cosine, sine)
    sent = pl.pallas_call(
        lift_other_kernel,
        name="lift_other",
        out_shape=jax.ShapeDtypeStruct((4, 8, 2, 8, 384), BF),
        in_specs=[VM] * 7,
        out_specs=VM,
        compiler_params=params(),
    )(first, rows, got, other, lists, cosine, sine)
    moved = exchange(sent.reshape(64, 8, 384), "clus")

    sent = pl.pallas_call(
        translate_kernel,
        name="translate",
        out_shape=jax.ShapeDtypeStruct((32, 2, 8, 256), BF),
        in_specs=[VM],
        out_specs=VM,
        scratch_shapes=[
            pltpu.VMEM((256, 512), BF),
            pltpu.VMEM((256, 128), jnp.int32),
            pltpu.VMEM((128, 512), BF),
            pltpu.VMEM((256, 256), F32),
            pltpu.VMEM((256, 256), F32),
        ],
        compiler_params=params(),
    )(moved.reshape(32, 2, 8, 384))
    moved = exchange(sent.reshape(64, 8, 256), "clus")

    sent = pl.pallas_call(
        descend_kernel,
        name="descend",
        out_shape=jax.ShapeDtypeStruct((8, 64, 256), BF),
        in_specs=[SM, VM, VM, VM, VM, VM],
        out_specs=VM,
        scratch_shapes=[
            pltpu.VMEM((8, 512, 256), BF),
            pltpu.VMEM((512, 256), F32),
        ],
        compiler_params=params(),
    )(child_slot, moved.reshape(4, 8, 2, 8, 256), half, other, cosine, sine)
    got = exchange(sent, "samp")

    return pl.pallas_call(
        finish_kernel,
        name="finish",
        out_shape=jax.ShapeDtypeStruct((4, 128, 128), BF),
        in_specs=[VM, VM, VM],
        out_specs=VM,
        compiler_params=params(),
    )(got, radiate, near)


def solution(mesh):
    in_specs = (
        P("clus", None, None),
        P(("clus", "samp"), None, None, None),
        P(("clus", "samp"), None, None, None, None),
        P(("clus", "samp"), None),
        P("clus"),
        P("samp", None),
        P(),
        P("clus", None),
        P("clus", None),
        P("clus", None),
        P(None, None, "samp"),
    )
    out_specs = P(("clus", "samp"), None, None)
    return jax.shard_map(body, mesh=mesh, in_specs=in_specs, out_specs=out_specs, check_vma=False)
```

```python
import jax
import jax.numpy as jnp
from jax import lax
from jax.experimental import pallas as pl
from jax.experimental.pallas import tpu as pltpu
from jax.sharding import PartitionSpec as P

BF = jnp.bfloat16
F32 = jnp.float32
VMEM_LIMIT = 16 * 1024 * 1024
VM = pl.BlockSpec(memory_space=pltpu.VMEM)
SM = pl.BlockSpec(memory_space=pltpu.SMEM)


def nt_dot(a, b):
    return lax.dot_general(a, b, (((1,), (1,)), ((), ())), preferred_element_type=F32)


def nn_dot(a, b):
    return lax.dot_general(a, b, (((1,), (0,)), ((), ())), preferred_element_type=F32)


def tn_dot(a, b):
    return lax.dot_general(a, b, (((0,), (0,)), ((), ())), preferred_element_type=F32)


def rows_of(shape, dim):
    return lax.broadcasted_iota(jnp.int32, shape, dim)


def radiate_kernel(cur, rad_all, itp, out, own, rad, half, data, in_sems, out_sems):
    clus = lax.axis_index("clus")
    mine = pl.ds(pl.multiple_of(lax.rem(clus, 2) * 128, 128), 128)
    pairs = [
        (itp.at[mine], half),
        (cur.at[pl.ds(lax.axis_index("samp") * 4, 4)], own),
    ] + [(rad_all.at[c], rad.at[c]) for c in range(4)]
    copies = [pltpu.make_async_copy(a, b, in_sems.at[i]) for i, (a, b) in enumerate(pairs)]
    for copy in copies:
        copy.start()
    copies[0].wait()
    sends = [
        pltpu.make_async_copy(half, out.at[s, 64:192, :], out_sems.at[s]) for s in range(8)
    ]
    for send in sends:
        send.start()
    copies[1].wait()
    for c in range(4):
        copies[2 + c].wait()
        values = own[c].astype(F32).T.astype(BF)
        with_real = nt_dot(values, rad[c, 0])
        with_imag = nt_dot(values, rad[c, 1])
        real = with_real[:64] - with_imag[64:]
        imag = with_real[64:] + with_imag[:64]
        for s in range(8):
            both = jnp.concatenate([real[8 * s : 8 * s + 8], imag[8 * s : 8 * s + 8]], axis=0)
            data[s, 16 * c : 16 * c + 16, :] = both.astype(BF)
    last = pltpu.make_async_copy(data, out.at[:, 0:64, :], out_sems.at[8])
    last.start()
    for send in sends:
        send.wait()
    last.wait()


def own_lanes(k):
    core = lax.rem(lax.axis_index("clus"), 2)
    return pl.ds(pl.multiple_of(k * 256 + core * 128, 128), 128)


def other_lanes(k):
    core = lax.rem(lax.axis_index("clus"), 2)
    return pl.ds(pl.multiple_of(k * 256 + (1 - core) * 128, 128), 128)


def lift_halves(rows, matrix, cosines, sines):
    reals, imags = ([], []), ([], [])
    for p in range(4):
        lifted = nt_dot(rows[128 * p : 128 * p + 128, :], matrix)
        for h in range(2):
            lanes = slice(128 * h, 128 * h + 128)
            real_sum = imag_sum = None
            for o in range(8):
                re = lifted[16 * o : 16 * o + 8, lanes]
                im = lifted[16 * o + 8 : 16 * o + 16, lanes]
                co, si = cosines[h][o : o + 1], sines[h][o : o + 1]
                real = re * co - im * si
                imag = re * si + im * co
                real_sum = real if real_sum is None else real_sum + real
                imag_sum = imag if imag_sum is None else imag_sum + imag
            reals[h].append(real_sum)
            imags[h].append(imag_sum)
    stacks = [jnp.stack(reals[h] + imags[h], axis=0) for h in range(2)]
    return [jnp.swapaxes(stack, 0, 1).astype(BF) for stack in stacks]


def lift_own_kernel(slots, got, cosine, sine, out, rows, inverse):
    for c in range(32):
        inverse[slots[c]] = c
    for n in range(32):
        c = inverse[n]
        src = pl.multiple_of(lax.rem(c, 4) * 16, 16)
        rows[16 * n : 16 * n + 16, :] = got[lax.div(c, 4), pl.ds(src, 16), :]
    for k in range(0, 8, 2):
        lanes = [own_lanes(k), own_lanes(k + 1)]
        matrix = jnp.concatenate([got[k, 64:192, :], got[k + 1, 64:192, :]], axis=0)
        cosines = [cosine[:, at] for at in lanes]
        sines = [sine[:, at] for at in lanes]
        blocks = lift_halves(rows, matrix, cosines, sines)
        for h in range(2):
            for r in range(8):
                out[r // 2, k + h, r % 2] = blocks[h][r]


def lift_other_kernel(first, rows, other, lists, cosine, sine, out):
    tile = lists[...].astype(BF)
    for k in range(0, 8, 2):
        lanes = [other_lanes(k), other_lanes(k + 1)]
        matrix = jnp.concatenate([other[k], other[k + 1]], axis=0)
        cosines = [cosine[:, at] for at in lanes]
        sines = [sine[:, at] for at in lanes]
        blocks = lift_halves(rows, matrix, cosines, sines)
        for h in range(2):
            for r in range(8):
                out[r // 2, k + h, r % 2, :, 0:128] = first[r // 2, k + h, r % 2]
                out[r // 2, k + h, r % 2, :, 128:256] = blocks[h][r]
                out[r // 2, k + h, r % 2, :, 256:384] = tile


def translate_kernel(got, tran, out, table, codes, real_acc, imag_acc):
    def uppers(even, odd):
        low = rows_of(even.shape, 1) < 4
        return jnp.where(low, even, pltpu.roll(odd, 4, 1)).reshape(256, even.shape[2])

    def lowers(even, odd):
        low = rows_of(even.shape, 1) < 4
        return jnp.where(low, pltpu.roll(even, 4, 1), odd).reshape(256, even.shape[2])

    for h in range(2):
        even = got[:, 0, :, 128 * h : 128 * h + 128].astype(F32)
        odd = got[:, 1, :, 128 - 128 * h : 256 - 128 * h].astype(F32)
        table[:, 128 * h : 128 * h + 128] = uppers(even, odd).astype(BF)
        table[:, 256 + 128 * h : 384 + 128 * h] = lowers(even, odd).astype(BF)
    even = got[:, 0, :, 256:384].astype(F32)
    odd = got[:, 1, :, 256:384].astype(F32)
    codes[...] = uppers(even, odd).astype(jnp.int32)
    col = rows_of((256, 256), 1)
    kinds = rows_of((256, 64), 1)
    for first in range(0, 16, 4):
        picks = [(col == codes[:, first + f : first + f + 1]).astype(F32) for f in range(4)]
        turns = [(kinds == codes[:, 16 + first + f : 17 + first + f]).astype(F32) for f in range(4)]
        both = nn_dot(jnp.concatenate([p.astype(BF) for p in picks], axis=0), table[...])
        factor = nn_dot(jnp.concatenate([t.astype(BF) for t in turns], axis=0), tran[...])
        real = imag = None
        for f in range(4):
            rows = slice(256 * f, 256 * f + 256)
            re, im = both[rows, :256], both[rows, 256:]
            tre, tim = factor[rows, :256], factor[rows, 256:]
            add_real = re * tre - im * tim
            add_imag = re * tim + im * tre
            real = add_real if real is None else real + add_real
            imag = add_imag if imag is None else imag + add_imag
        if first == 0:
            real_acc[...] = real
            imag_acc[...] = imag
        else:
            real_acc[...] += real
            imag_acc[...] += imag
    low = rows_of((32, 8, 256), 1) < 4
    re = real_acc[...].reshape(32, 8, 256)
    im = imag_acc[...].reshape(32, 8, 256)
    out[:, 0] = jnp.where(low, re, pltpu.roll(im, 4, 1)).astype(BF)
    last = jnp.where(low, pltpu.roll(re, 4, 1), im).astype(BF)
    out[:, 1, :, 0:128] = last[:, :, 128:256]
    out[:, 1, :, 128:256] = last[:, :, 0:128]


def descend_kernel(slots, got, half, other, cosine, sine, out, lhs, acc):
    for k in range(8):
        block = jnp.stack([got[r // 2, k, r % 2].astype(F32) for r in range(8)], axis=0)
        block = jnp.swapaxes(block, 0, 1)
        for h, at in enumerate((own_lanes(k), other_lanes(k))):
            lanes = slice(128 * h, 128 * h + 128)
            cos, sin = cosine[:, at], sine[:, at]
            for o in range(8):
                co = jnp.broadcast_to(cos[o : o + 1], (8, 128))
                si = jnp.broadcast_to(sin[o : o + 1], (8, 128))
                for p in range(4):
                    re, im = block[p][:, lanes], block[4 + p][:, lanes]
                    both = jnp.concatenate([re * co + im * si, im * co - re * si], axis=0)
                    n = 8 * p + o
                    lhs[k, 16 * n : 16 * n + 16, lanes] = both.astype(BF)
    for first in range(0, 512, 256):
        total = None
        for k in range(8):
            whole = jnp.concatenate([half[k], other[k]], axis=0)
            part = nn_dot(lhs[k, first : first + 256, :], whole)
            total = part if total is None else total + part
        acc[first : first + 256, :] = total
    for c in range(32):
        src = pl.multiple_of(slots[c] * 16, 16)
        out[c // 4, 16 * (c % 4) : 16 * (c % 4) + 16, :] = acc[pl.ds(src, 16), :].astype(BF)


def finish_kernel(got, rad, near, out):
    for c in range(4):
        pieces = [got[s, 16 * c : 16 * c + 16, :].astype(F32) for s in range(8)]
        rows = jnp.concatenate([q[:8] for q in pieces] + [q[8:] for q in pieces], axis=0)
        received = rows.T.astype(BF)
        with_real = tn_dot(rad[c, 0], received)
        with_imag = tn_dot(rad[c, 1], received)
        turned = pltpu.roll(with_imag, 64, 1)
        lane = rows_of((128, 128), 1)
        far = with_real + jnp.where(lane < 64, turned, -turned)
        out[c] = (near[c] + far).astype(BF)


def params(limit=VMEM_LIMIT):
    return pltpu.CompilerParams(vmem_limit_bytes=limit)


def near_kernel(cols, low, cur, high, blocks, out, window, sems):
    pairs = [(low, window.at[0:8]), (cur, window.at[8:40]), (high, window.at[40:48])]
    copies = [pltpu.make_async_copy(a, b, sems.at[i]) for i, (a, b) in enumerate(pairs)]
    for copy in copies:
        copy.start()
    for copy in copies:
        copy.wait()
    start = lax.axis_index("clus") * 32 - 8

    def row(c, carry):
        total = None
        for j in range(10):
            part = nn_dot(blocks[c, j].reshape(256, 128), window[cols[c, j] - start])
            total = part if total is None else total + part
        turned = pltpu.roll(total[128:], 64, 1)
        lane = rows_of((128, 128), 1)
        out[c] = total[:128] + jnp.where(lane < 64, -turned, turned)
        return carry

    lax.fori_loop(0, 4, row, 0)


def halo(currents):
    up = [(i, i + 1) for i in range(lax.axis_size("clus") - 1)]
    down = [(b, a) for a, b in up]
    return lax.ppermute(currents[24:32], "clus", up), lax.ppermute(currents[0:8], "clus", down)


def near_field(currents, low, high, near_blocks, near_cols):
    hbm = pl.BlockSpec(memory_space=pltpu.HBM)
    return pl.pallas_call(
        near_kernel,
        name="near",
        out_shape=jax.ShapeDtypeStruct((4, 128, 128), F32),
        in_specs=[SM, hbm, hbm, hbm, VM],
        out_specs=VM,
        scratch_shapes=[pltpu.VMEM((48, 128, 128), BF), pltpu.SemaphoreType.DMA((3,))],
        cost_estimate=pl.CostEstimate(flops=168000000, bytes_accessed=4600000, transcendentals=0),
        compiler_params=params(),
    )(near_cols, low, currents, high, near_blocks)


def body(
    currents,
    radiate,
    near_blocks,
    near_cols,
    child_slot,
    interp,
    shift_angle,
    far_dev,
    far_loc,
    far_type,
    transl,
):
    partner = [(i, i ^ 1) for i in range(lax.axis_size("clus"))]
    exchange = lambda x, axis: lax.all_to_all(x, axis, split_axis=0, concat_axis=0, tiled=True)
    lists = jnp.pad((far_dev * 4 + far_loc).astype(F32), ((0, 4), (0, 112)))
    lists = lists + jnp.pad(far_type.astype(F32), ((0, 4), (16, 96)))
    cosine = jnp.cos(shift_angle)
    sine = jnp.sin(shift_angle)

    sent = pl.pallas_call(
        radiate_kernel,
        name="radiate",
        out_shape=jax.ShapeDtypeStruct((8, 192, 256), BF),
        in_specs=[pl.BlockSpec(memory_space=pltpu.HBM)] * 3,
        out_specs=pl.BlockSpec(memory_space=pltpu.HBM),
        scratch_shapes=[
            pltpu.VMEM((4, 128, 128), BF),
            pltpu.VMEM((4, 2, 256, 128), BF),
            pltpu.VMEM((128, 256), BF),
            pltpu.VMEM((8, 64, 256), BF),
            pltpu.SemaphoreType.DMA((6,)),
            pltpu.SemaphoreType.DMA((9,)),
        ],
        compiler_params=params(60 * 1024 * 1024),
    )(currents, radiate, interp)
    sent, mine, slices = lax.optimization_barrier((sent, currents, transl))
    got = exchange(sent, "samp")
    swap = []
    for clus in range(64):
        for samp in range(8):
            taker = (clus // 16) * 16 + samp * 2 + clus % 2
            swap.append((clus * 8 + samp, taker * 8 + (clus // 2) % 8))
    tran = lax.ppermute(slices, ("clus", "samp"), swap).reshape(64, 512)
    low, high = halo(mine)
    near = near_field(mine, low, high, near_blocks, near_cols)
    early = (got, near, tran, cosine, sine, lists)
    got, near, tran, cosine, sine, lists = lax.optimization_barrier(early)
    half = got[:, 64:192]
    other = lax.ppermute(half, "clus", partner)

    first, rows = pl.pallas_call(
        lift_own_kernel,
        name="lift_own",
        out_shape=(
            jax.ShapeDtypeStruct((4, 8, 2, 8, 128), BF),
            jax.ShapeDtypeStruct((512, 256), BF),
        ),
        in_specs=[SM, VM, VM, VM],
        out_specs=(VM, VM),
        scratch_shapes=[pltpu.SMEM((32,), jnp.int32)],
        compiler_params=params(),
    )(child_slot, got, cosine, sine)
    sent = pl.pallas_call(
        lift_other_kernel,
        name="lift_other",
        out_shape=jax.ShapeDtypeStruct((4, 8, 2, 8, 384), BF),
        in_specs=[VM] * 6,
        out_specs=VM,
        compiler_params=params(),
    )(first, rows, other, lists, cosine, sine)
    moved = exchange(sent.reshape(64, 8, 384), "clus")

    sent = pl.pallas_call(
        translate_kernel,
        name="translate",
        out_shape=jax.ShapeDtypeStruct((32, 2, 8, 256), BF),
        in_specs=[VM, VM],
        out_specs=VM,
        scratch_shapes=[
            pltpu.VMEM((256, 512), BF),
            pltpu.VMEM((256, 128), jnp.int32),
            pltpu.VMEM((256, 256), F32),
            pltpu.VMEM((256, 256), F32),
        ],
        compiler_params=params(),
    )(moved.reshape(32, 2, 8, 384), tran)
    moved = exchange(sent.reshape(64, 8, 256), "clus")

    sent = pl.pallas_call(
        descend_kernel,
        name="descend",
        out_shape=jax.ShapeDtypeStruct((8, 64, 256), BF),
        in_specs=[SM, VM, VM, VM, VM, VM],
        out_specs=VM,
        scratch_shapes=[
            pltpu.VMEM((8, 512, 256), BF),
            pltpu.VMEM((512, 256), F32),
        ],
        compiler_params=params(),
    )(child_slot, moved.reshape(4, 8, 2, 8, 256), half, other, cosine, sine)
    got = exchange(sent, "samp")

    return pl.pallas_call(
        finish_kernel,
        name="finish",
        out_shape=jax.ShapeDtypeStruct((4, 128, 128), BF),
        in_specs=[VM, VM, VM],
        out_specs=VM,
        compiler_params=params(),
    )(got, radiate, near)


def solution(mesh):
    in_specs = (
        P("clus", None, None),
        P(("clus", "samp"), None, None, None),
        P(("clus", "samp"), None, None, None, None),
        P(("clus", "samp"), None),
        P("clus"),
        P("samp", None),
        P(),
        P("clus", None),
        P("clus", None),
        P("clus", None),
        P(None, None, "samp"),
    )
    out_specs = P(("clus", "samp"), None, None)
    return jax.shard_map(body, mesh=mesh, in_specs=in_specs, out_specs=out_specs, check_vma=False)
```
